512 devices in a mesh: dp: 64 (over x, y, z_lo), tensor: 8 (over z_hi, core).
Axes of the slice: x: 4, y: 4, z: 16 (z_hi: 4, z_lo: 4; z = z_hi * 4 + z_lo), core: 2. Of those that a mesh axis runs over, the one named last changes fastest.
Arguments:
- normed: bfloat16 [4096, 1280], P('dp'), may hold values from -6 to 6
- residual_in: bfloat16 [4096, 1280], P('dp'), may hold values from -6 to 6
- w_up: bfloat16 [1280, 5120], P('dp', 'tensor'), may hold values from -0.15625 to 0.15625
- w_down: bfloat16 [5120, 1280], P('tensor', 'dp'), may hold values from -0.15625 to 0.15625
- final_gain: float32 [1280], replicated, may hold values from 0.1 to 1.9
- head_cols: bfloat16 [1280, 16], replicated, may hold values from -4 to 4
- sub_inputs: int32 [8192], P('tensor'), may hold values from 0 to 1279
- sub_hidden: int32 [8192], P('tensor'), may hold values from 0 to 5119, as said below
- panels: bfloat16 [2, 256, 8192], P(None, 'dp', 'tensor'), may hold values from -0.1001 to 0.1001, as said below
- inverses: bfloat16 [2, 256, 256], replicated, may hold values from -0.1001 to 2, as said below
Outputs:
- whitened: bfloat16 [4096, 16, 8192], P('dp', None, 'tensor')
The draws below stay inside these ranges and needn't reach their ends.
Inputs may be any that keep to these rules, and one draw needn't show every extreme that they name: `sub_hidden`: window rows t * 1024 to (t + 1) * 1024 - 1 name hidden units t * 640 to (t + 1) * 640 - 1. `panels`: entry [q, c, r] is zero for r < (q + 1) * 256. `inverses`: each block is lower triangular with a positive diagonal.
All inputs are finite; a program needn't handle non-finite values.
Results may differ from the reference program's by a relative error of at most 0.0069.
Values may be sent and summed in bfloat16 or wider, within the bound.
No kernel may reach another device: no remote copies, remote signals or barrier semaphores. Data moves between devices by JAX's collectives and lax.ppermute only.
A program may use at most 64 MiB of HBM per device.

```python
import math
import jax
import jax.numpy as jnp
from jax import lax

D = 1280
FF = 5120
LOGITS = 16
PANEL = 256
IMG_DEV = 64
ROWS_T = 1024
FF_T = 640
WROWS = 8192
IMGS = 4096


def draw_sub_hidden(key, part):
    row_ids = jnp.arange(WROWS, dtype=jnp.int32)
    owner = row_ids // ROWS_T
    within = row_ids % ROWS_T
    picked = jax.random.randint(key, (WROWS,), 0, FF_T, dtype=jnp.int32)
    picked = jnp.where(within == 0, 0, jnp.where(within == 1, FF_T - 1, picked))
    return (owner * FF_T + picked).astype(jnp.int32)


def draw_panels(key, part):
    key_vals = jax.random.fold_in(jax.random.fold_in(key, 11), 0)
    values = jax.random.uniform(key_vals, (2, PANEL, WROWS), jnp.float32, -0.1, 0.1)
    row_ids = jnp.arange(WROWS, dtype=jnp.int32)[None, None, :]
    which = jnp.arange(2, dtype=jnp.int32)[:, None, None]
    values = jnp.where(row_ids >= (which + 1) * PANEL, values, 0.0)
    return values.astype(jnp.bfloat16)


def draw_inverses(key, part):
    key_diag, key_off = jax.random.split(jax.random.fold_in(key, 23))
    diag_vals = jnp.exp(jax.random.uniform(key_diag, (2, PANEL), jnp.float32, math.log(0.5), math.log(2.0)))
    off_vals = jax.random.uniform(key_off, (2, PANEL, PANEL), jnp.float32, -0.1, 0.1)
    row_ids = jnp.arange(PANEL, dtype=jnp.int32)[:, None]
    col_ids = jnp.arange(PANEL, dtype=jnp.int32)[None, :]
    lower = (row_ids > col_ids)[None, :, :]
    diagonal = (row_ids == col_ids)[None, :, :]
    values = jnp.where(lower, off_vals, 0.0) + jnp.where(diagonal, diag_vals[:, :, None], 0.0)
    return values.astype(jnp.bfloat16)


def place_ends(values, own_key, least, largest):
    longest = values.shape.index(max(values.shape))
    spots = []
    for shift in (0, 1):
        where = [jax.random.randint(jax.random.fold_in(own_key, axis), (), 0, length) for axis, length in enumerate(values.shape)]
        where[longest] = (where[longest] + shift) % values.shape[longest]
        spots.append(tuple(where))
    return values.at[spots[0]].set(least).at[spots[1]].set(largest)


def block_scale(stream_key, dims, shards, low, largest):
    def one(axis_at, blocks):
        draws = jax.random.uniform(jax.random.fold_in(jax.random.fold_in(stream_key, 6), axis_at), (blocks,), jnp.float32, low / len(shards), largest / len(shards))
        return jnp.repeat(jnp.exp(draws), dims[axis_at] // blocks).reshape((-1,) + (1,) * (len(dims) - axis_at - 1))

    factor_of = one(*shards[0])
    for cut in shards[1:]:
        factor_of = factor_of * one(*cut)
    return factor_of


def noise(rng, shape, spread, limit, cuts=(), held_as=jnp.bfloat16):
    loudness = block_scale(rng, shape, cuts, -0.22, 0.18) if cuts else 1.0
    values = jax.random.normal(rng, shape, jnp.float32) * spread * loudness
    return jnp.minimum(jnp.maximum(values, -limit), limit).astype(held_as)


def setup_inputs(seed: int = 0) -> dict:
    splits = jax.random.split(jax.random.key(seed), 11)
    return {
        "normed": noise(splits[0], (IMGS, D), 1.0, 6.0, ((0, 64),)),
        "residual_in": noise(splits[1], (IMGS, D), 1.0, 6.0, ((0, 64),)),
        "w_up": noise(splits[2], (D, FF), D ** -0.5, 0.15625, ((0, 64), (1, 8))),
        "w_down": noise(splits[3], (FF, D), D ** -0.5, 0.15625, ((0, 8), (1, 64))),
        "final_gain": jnp.clip(1.0 + 0.18 * jax.random.normal(splits[4], (D,), jnp.float32), 0.1, 1.9),
        "head_cols": noise(splits[5], (D, LOGITS), 1.0, 4.0),
        "sub_inputs": place_ends(jax.random.randint(splits[6], (WROWS,), 0, D), jax.random.fold_in(splits[6], 1), 0, D - 1).astype(jnp.int32),
        "sub_hidden": draw_sub_hidden(jax.random.fold_in(splits[10], 71), 0),
        "panels": draw_panels(jax.random.fold_in(splits[10], 71), 0),
        "inverses": draw_inverses(jax.random.fold_in(splits[10], 71), 0),
    }


def gelu_parts(values):
    normal_cdf = 0.5 * (1.0 + jax.scipy.special.erf(values * 0.7071067811865476))
    slope = normal_cdf + values * jnp.exp(-0.5 * values * values) * 0.3989422804014327
    return (values * normal_cdf, slope)

def logit_adjoint(block_result, final_gain, head_cols):
    mean_x = lax.optimization_barrier(jnp.mean(block_result, axis=1, keepdims=True))
    centred_rows = block_result - mean_x
    inverse_deviation = lax.rsqrt(lax.optimization_barrier(jnp.mean(centred_rows * centred_rows, axis=1, keepdims=True)) + 1e-06)
    normalized_input = centred_rows * inverse_deviation
    head_scaled_rows = final_gain[:, None] * head_cols.astype(jnp.float32)
    head_average = lax.optimization_barrier(jnp.mean(head_scaled_rows, axis=0))
    project_rows = jnp.dot(normalized_input, head_scaled_rows, precision=lax.Precision.HIGHEST) / block_result.shape[1]
    return inverse_deviation[:, :, None] * (head_scaled_rows.T[None, :, :] - head_average[None, :, None] - normalized_input[:, None, :] * project_rows[:, :, None])

def apply_inverse(block, inverse):
    return lax.dot_general(block, inverse, (((1,), (1,)), ((), ())), preferred_element_type=jnp.float32)

def reference(normed, residual_in, w_up, w_down, final_gain, head_cols, sub_inputs, sub_hidden, panels, inverses):

    def one_block(first_row):
        inputs = lax.dynamic_slice_in_dim(normed, first_row, IMG_DEV, 0)
        before = lax.dynamic_slice_in_dim(residual_in, first_row, IMG_DEV, 0)
        up_pre = jnp.dot(inputs, w_up, preferred_element_type=jnp.float32)
        activ, slope = gelu_parts(up_pre)
        hidden = activ.astype(jnp.bfloat16)
        block_result = before.astype(jnp.float32) + jnp.dot(hidden, w_down, preferred_element_type=jnp.float32)
        adjoint = logit_adjoint(block_result, final_gain, head_cols).astype(jnp.bfloat16)
        back = lax.dot_general(adjoint.reshape(IMG_DEV * LOGITS, D), w_down, (((1,), (1,)), ((), ())), preferred_element_type=jnp.float32)
        delta = back.reshape(IMG_DEV, LOGITS, FF) * slope[:, None, :]
        picked = jnp.take(inputs, sub_inputs, axis=1).astype(jnp.float32)
        jac = (picked[:, None, :] * jnp.take(delta, sub_hidden, axis=2)).astype(jnp.bfloat16)
        jac = jac.reshape(IMG_DEV * LOGITS, WROWS)
        first = apply_inverse(jac[:, :PANEL], inverses[0]).astype(jnp.bfloat16)
        carry = jnp.dot(first, panels[0], preferred_element_type=jnp.float32)
        second_in = (jac[:, PANEL:2 * PANEL].astype(jnp.float32) - carry[:, PANEL:2 * PANEL]).astype(jnp.bfloat16)
        second = apply_inverse(second_in, inverses[1]).astype(jnp.bfloat16)
        update = carry + jnp.dot(second, panels[1], preferred_element_type=jnp.float32)
        below = (jac.astype(jnp.float32) - update).astype(jnp.bfloat16)
        result = jnp.concatenate([first, second, below[:, 2 * PANEL:]], axis=1)
        return result.reshape(IMG_DEV, LOGITS, WROWS)
    starts = jnp.arange(IMGS // IMG_DEV, dtype=jnp.int32) * IMG_DEV
    return lax.map(one_block, starts).reshape(IMGS, LOGITS, WROWS)
```

```python
import jax
import jax.numpy as jnp
from jax import lax
from jax.experimental import pallas as pl
from jax.experimental.pallas import tpu as pltpu
from jax.sharding import Mesh, PartitionSpec as P

DP = ("x", "y", "zl")
TENSOR = ("zh", "c")
F32 = jnp.float32
BF16 = jnp.bfloat16
STEP = 16


def gelu_parts(values):
    normal_cdf = 0.5 * (1.0 + jax.scipy.special.erf(values * 0.7071067811865476))
    slope = normal_cdf + values * jnp.exp(-0.5 * values * values) * 0.3989422804014327
    return (values * normal_cdf, slope)


def swap_core(values):
    return lax.ppermute(values, "c", [(0, 1), (1, 0)])


def gather_by_sends(shard, axis, count):
    spread = jnp.broadcast_to(shard[None], (count,) + shard.shape)
    return lax.all_to_all(spread, axis, 0, 0)


def ring_gather(shard, axis, count):
    ahead = [shard] + [
        lax.ppermute(shard, axis, [(i, (i - k) % count) for i in range(count)]) for k in range(1, count)
    ]
    twice = jnp.concatenate([part[None] for part in ahead + ahead[:-1]], axis=0)
    start = (count - lax.axis_index(axis)) % count
    return lax.dynamic_slice_in_dim(twice, start, count, 0)


def split2(values):
    high = lax.reduce_precision(values, 8, 7)
    return high.astype(BF16), (values - high).astype(BF16)


def dot32(lhs, rhs):
    return jnp.dot(lhs, rhs, preferred_element_type=F32)


def dot_t(lhs, rhs):
    return lax.dot_general(lhs, rhs, (((1,), (1,)), ((), ())), preferred_element_type=F32)


def dot_split(values, rhs):
    rows = values.shape[0]
    both = dot32(jnp.concatenate(split2(values), axis=0), rhs)
    return both[:rows] + both[rows:]


def one_hot(index, depth):
    return (lax.broadcasted_iota(jnp.int32, (depth, index.shape[0]), 0) == index[None, :]).astype(BF16)


def middle_kernel(
    flag_ref, mine_ref, theirs_ref, normed_ref, picked_ref, head_ref, down_ref, extra_ref, inv_ref, share_ref, own_ref, mix_ref, up0, down0
):
    images, width = normed_ref.shape
    rows_dev = down_ref.shape[1]
    half = mix_ref.shape[1]
    logits = head_ref.shape[0] // 4
    places, sub = extra_ref.shape[0], extra_ref.shape[1]
    parts = width // (places * sub)
    at = 2 * rows_dev
    for place in range(places):
        for b in range(parts):
            row = (place * parts + b) * sub
            up0[row : row + sub, :] = extra_ref[place, :, at + b * half : at + (b + 1) * half]
            low = at + (parts + b) * half
            down0[row : row + sub, :] = extra_ref[place, :, low : low + half]
    _, slope0 = gelu_parts(dot32(normed_ref[...], up0[...]))
    mix_ref[:images, :] = slope0 * picked_ref[...]

    first_core = flag_ref[1] == 0
    mine, theirs = mine_ref[...], theirs_ref[...]
    block = jnp.concatenate([jnp.where(first_core, mine, theirs), jnp.where(first_core, theirs, mine)], axis=0)
    centred = block - jnp.mean(block, axis=1, keepdims=True)
    inv_std = lax.rsqrt(jnp.mean(centred * centred, axis=1, keepdims=True) + 1e-06)
    xhat = centred * inv_std
    inv_ref[...] = inv_std
    high = xhat.astype(BF16)
    low = (xhat - high.astype(F32)).astype(BF16)
    head = head_ref[...]
    both = jnp.concatenate([high, low], axis=0)
    share = dot_t(both, head[2 * logits :])
    share = share[:images] + share[images:]
    share_ref[...] = (share[:, :logits] + share[:, logits:]) / width
    lhs = jnp.concatenate([both, head[: 2 * logits]], axis=0)
    for rhs, out, base in ((down_ref, own_ref, 0), (down0, mix_ref, images)):
        product = dot32(lhs, rhs[...])
        out[base : base + images, :] = product[:images] + product[images : 2 * images]
        tail = product[2 * images :]
        out[base + images : base + images + logits, :] = tail[:logits] + tail[logits:]


def last_kernel(flag_ref, gain_ref, inv_ref, share_ref, own_ref, mine_ref, theirs_ref, inverse_ref, extra_ref, out_ref):
    images = gain_ref.shape[0]
    logits = share_ref.shape[1]
    rows_dev = gain_ref.shape[1]
    panel = inverse_ref.shape[1]
    first_image = pl.multiple_of(pl.program_id(0) * STEP, STEP)
    here = pl.ds(first_image, STEP)
    inv_std = inv_ref[here, :]
    diagonal = lax.broadcasted_iota(jnp.int32, (1, logits, logits), 1) == lax.broadcasted_iota(
        jnp.int32, (1, logits, logits), 2
    )
    share = jnp.sum(jnp.where(diagonal, share_ref[here, :][:, None, :], 0.0), axis=2, keepdims=True)

    def jacobian(gain, along, head):
        scale = gain * inv_std
        values = scale[:, None, :] * (head[None] - share * along[:, None, :])
        return values.reshape(STEP * logits, values.shape[2])

    def solved_side(side):
        is_mine = flag_ref[1] == side
        gain, along, head = (
            jnp.where(is_mine, mine_ref[rows, :], theirs_ref[rows, :])
            for rows in (here, pl.ds(images + first_image, STEP), slice(2 * images, 2 * images + logits))
        )
        return jacobian(gain, along, head)

    def inverted(values, inverse):
        high = values.astype(BF16)
        low = (values - high.astype(F32)).astype(BF16)
        return (dot_t(high, inverse) + dot_t(low, inverse)).astype(BF16)

    first = inverted(solved_side(0), inverse_ref[0])
    at = extra_ref.shape[2] - panel
    panel_01 = extra_ref[:, :, at:].reshape(panel, panel)
    second = inverted(solved_side(1) - dot32(first, panel_01), inverse_ref[1])
    own = jacobian(gain_ref[here, :], own_ref[here, :], own_ref[images : images + logits, :])
    panel_0 = extra_ref[:, :, :rows_dev].reshape(panel, rows_dev)
    panel_1 = extra_ref[:, :, rows_dev : 2 * rows_dev].reshape(panel, rows_dev)
    below = (own - (dot32(first, panel_0) + dot32(second, panel_1))).astype(BF16)
    out_ref[...] = below.reshape(out_ref.shape)

    @pl.when(flag_ref[0] == 1)
    def _():
        out_ref[:, :, :panel] = first.reshape(STEP, logits, panel)
        out_ref[:, :, panel : 2 * panel] = second.reshape(STEP, logits, panel)


def body(normed, residual_in, w_up, w_down, final_gain, head_cols, sub_inputs, sub_hidden, panels, inverses):
    images, width = normed.shape
    own, hidden_dev = w_up.shape
    logits = head_cols.shape[1]
    panel = inverses.shape[1]
    panel_dev = panels.shape[1]
    rows_dev = sub_inputs.shape[0]
    z_hi, core = lax.axis_index("zh"), lax.axis_index("c")
    rank = z_hi * 2 + core
    local_hidden = sub_hidden - rank * hidden_dev
    half = panel

    both = jnp.concatenate([w_up, w_down.T], axis=0)
    line = gather_by_sends(both, "zl", 4)
    line = jnp.concatenate(
        [line[:, :own].reshape(4 * own, hidden_dev), line[:, own:].reshape(4 * own, hidden_dev)], axis=0
    )
    plane = gather_by_sends(line, ("x", "y"), 16)
    up_full = plane[:, : 4 * own].reshape(width, hidden_dev)
    down_t = plane[:, 4 * own :].reshape(width, hidden_dev)

    later, hidden_first, inputs_first, panels_later, _ = lax.optimization_barrier(
        (both, local_hidden[: 2 * panel], sub_inputs[: 2 * panel], panels, line)
    )
    chosen = dot32(later, one_hot(hidden_first, hidden_dev)).astype(BF16)
    coded = jnp.stack([inputs_first // 128, inputs_first % 128]).astype(BF16)
    block01 = panels_later[0][:, panel : 2 * panel]
    sides = [
        jnp.concatenate([chosen[:, s * half : (s + 1) * half], block01, coded[:, s * half : (s + 1) * half]], axis=0)
        for s in range(2)
    ]
    payload = jnp.where(core == 0, sides[0], lax.ppermute(sides[1], "c", [(0, 1)]))
    sent = [lax.ppermute(payload, "zh", [(0, k)]) for k in (1, 2, 3)]
    payload = jnp.where(z_hi == 0, payload, sent[0] + sent[1] + sent[2])

    narrow = jnp.concatenate(
        [panels_later.reshape(2 * panel_dev * (rows_dev // half), half), payload[: 2 * own + panel_dev]], axis=0
    )
    narrow = ring_gather(narrow, "zl", 4)
    count = 2 * panel_dev * (rows_dev // half)
    line_panels = narrow[:, :count].reshape(4, 2, panel_dev, rows_dev)
    narrow = narrow[:, count:]
    chosen_up = narrow[:, :own].reshape(5, 16, half)
    chosen_down = narrow[:, own : 2 * own].reshape(5, 16, half)
    extra = jnp.concatenate(
        [line_panels[:, q].reshape(16, rows_dev) for q in range(2)]
        + [chosen_up[b] for b in range(5)]
        + [chosen_down[b] for b in range(5)]
        + [narrow[:, 2 * own :].reshape(16, half)],
        axis=1,
    )

    up_pre = dot32(normed, up_full)
    activ, slope = gelu_parts(up_pre)
    partial_out = dot_t(activ.astype(BF16), down_t)
    kept = lax.dynamic_slice_in_dim(partial_out, core * (images // 2), images // 2, 0)
    given = lax.dynamic_slice_in_dim(partial_out, (1 - core) * (images // 2), images // 2, 0)
    pair = kept + swap_core(given)
    peers = [lax.ppermute(pair, "zh", [(i, (i + k) % 4) for i in range(4)]) for k in (2, 1, 3)]

    spread = jnp.broadcast_to(extra[None], (16,) + extra.shape)
    spread, _ = lax.optimization_barrier((spread, plane[:, :1, :128]))
    extra = lax.all_to_all(spread, ("x", "y"), 0, 0)

    pick_own = one_hot(local_hidden, hidden_dev)
    down_own = dot32(down_t, pick_own).astype(BF16)
    gain_own = dot_split(slope, pick_own) * dot32(normed, one_hot(sub_inputs, width))
    index = payload[2 * own + panel_dev :].astype(jnp.int32)
    picked = dot32(normed, one_hot(index[0] * 128 + index[1], width))
    head = final_gain[:, None] * head_cols.astype(F32)
    centred_head = head - jnp.mean(head, axis=0)
    head_parts = jnp.concatenate(split2(centred_head.T) + split2(head.T), axis=0)

    mine = lax.dynamic_slice_in_dim(residual_in, core * (images // 2), images // 2, 0)
    block = mine.astype(F32) + ((pair + peers[0]) + (peers[1] + peers[2]))
    block_pair = swap_core(block)
    flag = jnp.stack([jnp.where(rank == 0, 1, 0), core]).astype(jnp.int32)

    vmem = pl.BlockSpec(memory_space=pltpu.VMEM)
    inv_std, share, own_products, mix = pl.pallas_call(
        middle_kernel,
        out_shape=(
            jax.ShapeDtypeStruct((images, 1), F32),
            jax.ShapeDtypeStruct((images, logits), F32),
            jax.ShapeDtypeStruct((images + logits, rows_dev), F32),
            jax.ShapeDtypeStruct((2 * images + logits, half), F32),
        ),
        in_specs=[pl.BlockSpec(memory_space=pltpu.SMEM)] + [vmem] * 7,
        out_specs=(vmem,) * 4,
        scratch_shapes=[pltpu.VMEM((width, half), BF16), pltpu.VMEM((width, half), BF16)],
        name="middle",
    )(flag, block, block_pair, normed, picked, head_parts, down_own, extra)
    mix_pair = swap_core(mix)
    return pl.pallas_call(
        last_kernel,
        grid=(images // STEP,),
        out_shape=jax.ShapeDtypeStruct((images, logits, rows_dev), BF16),
        in_specs=[pl.BlockSpec(memory_space=pltpu.SMEM)] + [vmem] * 8,
        out_specs=pl.BlockSpec((STEP, logits, rows_dev), lambda i: (i, 0, 0)),
        name="last",
    )(flag, gain_own, inv_std, share, own_products, mix, mix_pair, inverses, extra)


def solution(mesh):
    fine = Mesh(mesh.devices.reshape(4, 4, 4, 4, 2), ("x", "y", "zl", "zh", "c"))
    in_specs = (
        P(DP, None),
        P(DP, None),
        P(DP, TENSOR),
        P(TENSOR, DP),
        P(),
        P(),
        P(TENSOR),
        P(TENSOR),
        P(None, DP, TENSOR),
        P(),
    )
    out_specs = P(DP, None, TENSOR)

    return jax.shard_map(body, mesh=fine, in_specs=in_specs, out_specs=out_specs, check_vma=False)
```

```python
import jax
import jax.numpy as jnp
import numpy as np
from jax import lax
from jax.experimental import pallas as pl
from jax.experimental.pallas import tpu as pltpu
from jax.sharding import Mesh, PartitionSpec as P

DP = ("x", "y", "zl")
TENSOR = ("zh", "c")
F32 = jnp.float32
BF16 = jnp.bfloat16
STEP = 16
LIMIT = pltpu.CompilerParams(vmem_limit_bytes=16 * 1024 * 1024)


def gelu_parts(values):
    normal_cdf = 0.5 * (1.0 + jax.scipy.special.erf(values * 0.7071067811865476))
    slope = normal_cdf + values * jnp.exp(-0.5 * values * values) * 0.3989422804014327
    return (values * normal_cdf, slope)


def swap_core(values):
    return lax.ppermute(values, "c", [(0, 1), (1, 0)])


def gather_by_sends(shard, axis, count):
    spread = jnp.broadcast_to(shard[None], (count,) + shard.shape)
    return lax.all_to_all(spread, axis, 0, 0)


def ring_pieces(shard, axis, count):
    return [shard] + [
        lax.ppermute(shard, axis, [(i, (i - k) % count) for i in range(count)]) for k in range(1, count)
    ]


def weights_kernel(code_ref, line_ref, out_ref):
    pieces, rows, _ = line_ref.shape
    total = None
    for k in range(pieces):
        lane = lax.broadcasted_iota(jnp.int32, (code_ref.shape[0], rows), 1) + k * rows
        part = dot32((lane == code_ref[...]).astype(BF16), line_ref[k])
        total = part if total is None else total + part
    line = total.astype(BF16)
    for place in range(out_ref.shape[0]):
        out_ref[place] = line


def extra_kernel(flag_ref, device_ref, row_ref, p0, p1, p2, p3, out_ref):
    places, sub, _ = out_ref.shape
    rows, half = p0.shape
    code = jnp.bitwise_and(device_ref[...] - flag_ref[2], 3) * rows + row_ref[...]
    total = None
    for k, piece in enumerate((p0, p1, p2, p3)):
        lane = lax.broadcasted_iota(jnp.int32, (code.shape[0], rows), 1) + k * rows
        part = dot32((lane == code).astype(BF16), piece[...])
        total = part if total is None else total + part
    line = total.astype(BF16)
    for place in range(places):
        for b in range(line.shape[0] // sub):
            out_ref[place, :, b * half : (b + 1) * half] = line[b * sub : (b + 1) * sub, :]


def forward_kernel(flag_ref, normed_ref, plane_ref, pick_ref, picked_ref, kept_ref, given_ref, slope_ref, part):
    _, rows, hidden_dev = plane_ref.shape
    images, width = normed_ref.shape
    half_images = kept_ref.shape[0]
    half = pick_ref.shape[1] // 2
    up_pre = dot32(normed_ref[...], plane_ref[:, : rows // 2, :].reshape(width, hidden_dev))
    activ, slope = gelu_parts(up_pre)
    slope_ref[...] = slope
    down_t = plane_ref[:, rows // 2 :, :].reshape(width, hidden_dev)
    part[...] = dot_t(activ.astype(BF16), down_t)
    core = flag_ref[1]
    high = slope.astype(BF16)
    low = (slope - high.astype(F32)).astype(BF16)
    gain = dot32(jnp.concatenate([high, low], axis=0), pick_ref[...])
    gain = jnp.where(core == 0, (gain[:images] + gain[images:]) * picked_ref[...], 0.0)
    for out, side, at in ((kept_ref, core, 0), (given_ref, 1 - core, half)):
        out[:, :width] = part[pl.ds(pl.multiple_of(side * half_images, half_images), half_images), :]
        out[:, width : width + half] = gain[:half_images, at : at + half]
        out[:, width + half :] = gain[half_images:, at : at + half]


def split2(values):
    high = lax.reduce_precision(values, 8, 7)
    return high.astype(BF16), (values - high).astype(BF16)


def dot32(lhs, rhs):
    return jnp.dot(lhs, rhs, preferred_element_type=F32)


def dot_t(lhs, rhs):
    return lax.dot_general(lhs, rhs, (((1,), (1,)), ((), ())), preferred_element_type=F32)


def dot_split(values, rhs):
    rows = values.shape[0]
    both = dot32(jnp.concatenate(split2(values), axis=0), rhs)
    return both[:rows] + both[rows:]


def one_hot(index, depth):
    return (lax.broadcasted_iota(jnp.int32, (depth, index.shape[0]), 0) == index[None, :]).astype(BF16)


def solved_kernel(extra_ref, down_ref):
    width, half = down_ref.shape
    places, sub, lanes = extra_ref.shape
    parts = width // (places * sub)
    at = lanes - (parts + 1) * half
    for place in range(places):
        for b in range(parts):
            row = (place * parts + b) * sub
            down_ref[row : row + sub, :] = extra_ref[place, :, at + b * half : at + (b + 1) * half]


def middle_kernel(
    flag_ref, mine_ref, theirs_ref, head_ref, down_ref, down0_ref, down1_ref, inv_ref, share_ref, own_ref, mix_ref
):
    half_images = mine_ref.shape[0]
    width = head_ref.shape[1]
    images = 2 * half_images
    half = down0_ref.shape[1]
    logits = head_ref.shape[0] // 4
    first_core = flag_ref[1] == 0
    mine, theirs = mine_ref[:, :width], theirs_ref[:, :width]
    for side, source in ((flag_ref[1], mine_ref), (1 - flag_ref[1], theirs_ref)):
        mix_ref[side, :half_images, :] = source[:, width : width + half]
        mix_ref[side, half_images:images, :] = source[:, width + half :]
    block = jnp.concatenate([jnp.where(first_core, mine, theirs), jnp.where(first_core, theirs, mine)], axis=0)
    centred = block - jnp.mean(block, axis=1, keepdims=True)
    inv_std = lax.rsqrt(jnp.mean(centred * centred, axis=1, keepdims=True) + 1e-06)
    xhat = centred * inv_std
    inv_ref[...] = inv_std
    high = xhat.astype(BF16)
    low = (xhat - high.astype(F32)).astype(BF16)
    head = head_ref[...]
    both = jnp.concatenate([high, low], axis=0)
    share = dot_t(both, head[2 * logits :])
    share = share[:images] + share[images:]
    share_ref[...] = (share[:, :logits] + share[:, logits:]) / width
    lhs = jnp.concatenate([both, head[: 2 * logits]], axis=0)

    def write(rhs_ref, put):
        product = dot32(lhs, rhs_ref[...])
        tail = product[2 * images :]
        put(slice(0, images), product[:images] + product[images : 2 * images])
        put(slice(images, images + logits), tail[:logits] + tail[logits:])

    def put_own(rows, values):
        own_ref[rows, :] = values

    def put_mine(rows, values):
        mix_ref[flag_ref[1], images + rows.start : images + rows.stop, :] = values

    def put_theirs(rows, values):
        mix_ref[1 - flag_ref[1], images + rows.start : images + rows.stop, :] = values

    write(down_ref, put_own)
    write(down0_ref, put_mine)
    write(down1_ref, put_theirs)


def last_kernel(flag_ref, gain_ref, inv_ref, share_ref, own_ref, mix_ref, inverse_ref, extra_ref, out_ref):
    images = gain_ref.shape[0]
    logits = share_ref.shape[1]
    panel = inverse_ref.shape[1]
    first_image = pl.multiple_of(pl.program_id(0) * STEP, STEP)
    here = pl.ds(first_image, STEP)
    inv_std = inv_ref[here, :]
    diagonal = lax.broadcasted_iota(jnp.int32, (1, logits, logits), 1) == lax.broadcasted_iota(
        jnp.int32, (1, logits, logits), 2
    )
    share = jnp.sum(jnp.where(diagonal, share_ref[here, :][:, None, :], 0.0), axis=2, keepdims=True)

    def jacobian(gain, along, head):
        scale = gain * inv_std
        values = scale[:, None, :] * (head[None] - share * along[:, None, :])
        return values.reshape(STEP * logits, values.shape[2])

    def solved_side(side):
        along = mix_ref[side, pl.ds(images + first_image, STEP), :]
        return jacobian(mix_ref[side, here, :], along, mix_ref[side, 2 * images : 2 * images + logits, :])

    def inverted(values, inverse):
        high = values.astype(BF16)
        low = (values - high.astype(F32)).astype(BF16)
        return (dot_t(high, inverse) + dot_t(low, inverse)).astype(BF16)

    first = inverted(solved_side(0), inverse_ref[0])
    rows_dev = gain_ref.shape[1]
    panel_01 = extra_ref[:, :, extra_ref.shape[2] - panel :].reshape(panel, panel)
    second = inverted(solved_side(1) - dot32(first, panel_01), inverse_ref[1])
    own = jacobian(gain_ref[here, :], own_ref[here, :], own_ref[images : images + logits, :])
    panel_0 = extra_ref[:, :, :rows_dev].reshape(panel, rows_dev)
    panel_1 = extra_ref[:, :, rows_dev : 2 * rows_dev].reshape(panel, rows_dev)
    below = (own - (dot32(first, panel_0) + dot32(second, panel_1))).astype(BF16)
    out_ref[...] = below.reshape(out_ref.shape)

    @pl.when(flag_ref[0] == 1)
    def _():
        out_ref[:, :, :panel] = first.reshape(STEP, logits, panel)
        out_ref[:, :, panel : 2 * panel] = second.reshape(STEP, logits, panel)


def body(normed, residual_in, w_up, w_down, final_gain, head_cols, sub_inputs, sub_hidden, panels, inverses):
    images, width = normed.shape
    own, hidden_dev = w_up.shape
    logits = head_cols.shape[1]
    panel = inverses.shape[1]
    panel_dev = panels.shape[1]
    rows_dev = sub_inputs.shape[0]
    z_hi, core = lax.axis_index("zh"), lax.axis_index("c")
    rank = z_hi * 2 + core
    local_hidden = sub_hidden - rank * hidden_dev
    half = panel
    vmem = pl.BlockSpec(memory_space=pltpu.VMEM)
    smem = pl.BlockSpec(memory_space=pltpu.SMEM)
    flag = jnp.stack([jnp.where(rank == 0, 1, 0), core, lax.axis_index("zl")]).astype(jnp.int32)

    both = jnp.concatenate([w_up, w_down.T], axis=0)
    line = gather_by_sends(both, "zl", 4)
    row = np.arange(8 * own)
    code = row % (4 * own) // own * (2 * own) + row // (4 * own) * own + row % own
    line = pl.pallas_call(
        weights_kernel,
        out_shape=jax.ShapeDtypeStruct((16, 8 * own, hidden_dev), BF16),
        in_specs=[vmem] * 2,
        out_specs=vmem,
        compiler_params=LIMIT,
        name="merge_weights",
    )(code.astype(np.int32)[:, None], line)
    plane = lax.all_to_all(line, ("x", "y"), 0, 0)

    later, panels_later, hidden_first, inputs_later, _ = lax.optimization_barrier(
        (both[own:], panels, local_hidden[: 2 * panel], sub_inputs, line[0, :16, :128])
    )
    pick_first = one_hot(hidden_first, hidden_dev)
    chosen = dot32(later, pick_first).astype(BF16)
    block01 = panels_later[0][:, panel : 2 * panel]
    other = lax.ppermute(jnp.concatenate([chosen[:, half:], block01], axis=0), "c", [(0, 1)])
    payload = jnp.where(core == 0, jnp.concatenate([chosen[:, :half], block01], axis=0), other)
    sent = [lax.ppermute(payload, "zh", [(0, k)]) for k in (1, 2, 3)]
    payload = jnp.where(z_hi == 0, payload, sent[0] + sent[1] + sent[2])

    chunks = rows_dev // half
    narrow = jnp.concatenate([panels_later.reshape(2 * panel_dev * chunks, half), payload], axis=0)
    pieces = ring_pieces(narrow, "zl", 4)
    device, source = [], []
    for q in range(2):
        for b in range(chunks):
            device += [r // panel_dev for r in range(4 * panel_dev)]
            source += [(q * panel_dev + r % panel_dev) * chunks + b for r in range(4 * panel_dev)]
    at = 2 * panel_dev * chunks
    device += [r // own for r in range(4 * own)] + [r // panel_dev for r in range(4 * panel_dev)]
    source += [at + r % own for r in range(4 * own)] + [at + own + r % panel_dev for r in range(4 * panel_dev)]
    extra = pl.pallas_call(
        extra_kernel,
        out_shape=jax.ShapeDtypeStruct((16, 16, len(device) // 16 * half), BF16),
        in_specs=[smem] + [vmem] * 6,
        out_specs=vmem,
        compiler_params=LIMIT,
        name="merge_extra",
    )(flag, np.array(device, np.int32)[:, None], np.array(source, np.int32)[:, None], *pieces)
    extra = lax.all_to_all(extra, ("x", "y"), 0, 0)

    picked = dot32(normed, one_hot(inputs_later, width))
    kept, given, slope = pl.pallas_call(
        forward_kernel,
        out_shape=(
            jax.ShapeDtypeStruct((images // 2, width + 2 * half), F32),
            jax.ShapeDtypeStruct((images // 2, width + 2 * half), F32),
            jax.ShapeDtypeStruct((images, hidden_dev), F32),
        ),
        in_specs=[smem] + [vmem] * 4,
        out_specs=(vmem,) * 3,
        scratch_shapes=[pltpu.VMEM((images, width), F32)],
        compiler_params=LIMIT,
        name="forward",
    )(flag, normed, plane, pick_first, picked[:, : 2 * panel])
    pair = kept + swap_core(given)
    pair_sent = pair.astype(BF16)
    peers = [lax.ppermute(pair_sent, "zh", [(i, (i + k) % 4) for i in range(4)]) for k in (2, 1, 3)]

    pick_own = one_hot(local_hidden, hidden_dev)
    down_t = plane[:, 4 * own :].reshape(width, hidden_dev)
    down_own = dot32(down_t, pick_own).astype(BF16)
    gain_own = dot_split(slope, pick_own) * picked
    head = final_gain[:, None] * head_cols.astype(F32)
    centred_head = head - jnp.mean(head, axis=0)
    head_parts = jnp.concatenate(split2(centred_head.T) + split2(head.T), axis=0)

    peers = [peer.astype(F32) for peer in peers]
    mine = lax.dynamic_slice_in_dim(residual_in, core * (images // 2), images // 2, 0).astype(F32)
    block = mine + ((pair + peers[0]) + (peers[1] + peers[2]))[:, :width]
    solved_gain = [values[:, width:] for values in (pair, peers[1], peers[0], peers[2])]
    gain = jnp.where(z_hi == 0, solved_gain[0], solved_gain[1])
    gain = jnp.where(z_hi == 2, solved_gain[2], jnp.where(z_hi == 3, solved_gain[3], gain))
    block = jnp.concatenate([block, gain], axis=1)
    block_pair = swap_core(block)

    down_mine = pl.pallas_call(
        solved_kernel,
        out_shape=jax.ShapeDtypeStruct((width, half), BF16),
        in_specs=[vmem],
        out_specs=vmem,
        compiler_params=LIMIT,
        name="solved",
    )(extra)
    down_theirs = swap_core(down_mine)
    inv_std, share, own_products, mix = pl.pallas_call(
        middle_kernel,
        out_shape=(
            jax.ShapeDtypeStruct((images, 1), F32),
            jax.ShapeDtypeStruct((images, logits), F32),
            jax.ShapeDtypeStruct((images + logits, rows_dev), F32),
            jax.ShapeDtypeStruct((2, 2 * images + logits, half), F32),
        ),
        in_specs=[smem] + [vmem] * 6,
        out_specs=(vmem,) * 4,
        compiler_params=LIMIT,
        name="middle",
    )(flag, block, block_pair, head_parts, down_own, down_mine, down_theirs)
    return pl.pallas_call(
        last_kernel,
        grid=(images // STEP,),
        out_shape=jax.ShapeDtypeStruct((images, logits, rows_dev), BF16),
        in_specs=[smem] + [vmem] * 7,
        out_specs=pl.BlockSpec((STEP, logits, rows_dev), lambda i: (i, 0, 0)),
        compiler_params=LIMIT,
        name="last",
    )(flag, gain_own, inv_std, share, own_products, mix, inverses, extra)


def solution(mesh):
    fine = Mesh(mesh.devices.reshape(4, 4, 4, 4, 2), ("x", "y", "zl", "zh", "c"))
    in_specs = (
        P(DP, None),
        P(DP, None),
        P(DP, TENSOR),
        P(TENSOR, DP),
        P(),
        P(),
        P(TENSOR),
        P(TENSOR),
        P(None, DP, TENSOR),
        P(),
    )
    out_specs = P(DP, None, TENSOR)

    return jax.shard_map(body, mesh=fine, in_specs=in_specs, out_specs=out_specs, check_vma=False)
```

```python
import jax
import jax.numpy as jnp
import numpy as np
from jax import lax
from jax.experimental import pallas as pl
from jax.experimental.pallas import tpu as pltpu
from jax.sharding import Mesh, PartitionSpec as P

DP = ("x", "y", "zl")
TENSOR = ("zh", "c")
F32 = jnp.float32
BF16 = jnp.bfloat16
STEP = 32
LARGE = pltpu.CompilerParams(vmem_limit_bytes=60 * 1024 * 1024)
LIMIT = pltpu.CompilerParams(vmem_limit_bytes=20 * 1024 * 1024)


def gelu_parts(values):
    normal_cdf = 0.5 * (1.0 + jax.scipy.special.erf(values * 0.7071067811865476))
    slope = normal_cdf + values * jnp.exp(-0.5 * values * values) * 0.3989422804014327
    return (values * normal_cdf, slope)


def swap_core(values):
    return lax.ppermute(values, "c", [(0, 1), (1, 0)])


def gather_by_sends(shard, axis, count):
    spread = jnp.broadcast_to(shard[None], (count,) + shard.shape)
    return lax.all_to_all(spread, axis, 0, 0)


def ring_pieces(shard, axis, count):
    return [shard] + [
        lax.ppermute(shard, axis, [(i, (i - k) % count) for i in range(count)]) for k in range(1, count)
    ]


def weights_kernel(line_ref, out_ref, merged, done):
    pieces, rows, _ = line_ref.shape
    own = rows // 2
    shape = (pieces * rows, rows)
    row, source = (lax.broadcasted_iota(jnp.int32, shape, axis) for axis in (0, 1))
    total = None
    for k in range(pieces):
        target = source + k * own + jnp.where(source < own, 0, (pieces - 1) * own)
        part = dot32((row == target).astype(BF16), line_ref[k])
        total = part if total is None else total + part
    merged[...] = total.astype(BF16)
    send_copies(merged, out_ref, done)


def send_copies(merged, out_ref, done):
    copies = [pltpu.make_async_copy(merged, out_ref.at[place], done.at[place]) for place in range(out_ref.shape[0])]
    for copy in copies:
        copy.start()
    for copy in copies:
        copy.wait()


def extra_kernel(flag_ref, device_ref, row_ref, p0, p1, p2, p3, out_ref, merged, done):
    sub = merged.shape[0]
    rows, half = p0.shape
    code = jnp.bitwise_and(device_ref[...] - flag_ref[2], 3) * rows + row_ref[...]
    total = None
    for k, piece in enumerate((p0, p1, p2, p3)):
        lane = lax.broadcasted_iota(jnp.int32, (code.shape[0], rows), 1) + k * rows
        part = dot32((lane == code).astype(BF16), piece[...])
        total = part if total is None else total + part
    line = total.astype(BF16)
    for b in range(line.shape[0] // sub):
        merged[:, b * half : (b + 1) * half] = line[b * sub : (b + 1) * sub, :]
    send_copies(merged, out_ref, done)


def forward_kernel(flag_ref, normed_ref, plane_ref, index_ref, picked_ref, kept_ref, given_ref, slope_ref, part):
    _, rows, hidden_dev = plane_ref.shape
    images, width = normed_ref.shape
    half_images = kept_ref.shape[0]
    solved = index_ref.shape[1]
    half = solved // 2
    up_pre = dot32(normed_ref[...], plane_ref[:, : rows // 2, :].reshape(width, hidden_dev))
    activ, slope = gelu_parts(up_pre)
    slope_ref[...] = slope
    down_t = plane_ref[:, rows // 2 :, :].reshape(width, hidden_dev)
    part[...] = dot_t(activ.astype(BF16), down_t)
    core = flag_ref[1]
    high = slope.astype(BF16)
    low = (slope - high.astype(F32)).astype(BF16)
    pick = (lax.broadcasted_iota(jnp.int32, (hidden_dev, solved), 0) == index_ref[...]).astype(BF16)
    gain = dot32(jnp.concatenate([high, low], axis=0), pick)
    gain = jnp.where(core == 0, (gain[:images] + gain[images:]) * picked_ref[:, :solved], 0.0)
    for out, side, at in ((kept_ref, core, 0), (given_ref, 1 - core, half)):
        rows_here = pl.ds(pl.multiple_of(side * half_images, half_images), half_images)
        for run in range(2):
            base = run * (width // 2 + half)
            out[:, base : base + width // 2] = part[rows_here, run * (width // 2) : (run + 1) * (width // 2)]
            out[:, base + width // 2 : base + width // 2 + half] = gain[
                run * half_images : (run + 1) * half_images, at : at + half
            ]


def split2(values):
    high = lax.reduce_precision(values, 8, 7)
    return high.astype(BF16), (values - high).astype(BF16)


def dot32(lhs, rhs):
    return jnp.dot(lhs, rhs, preferred_element_type=F32)


def dot_t(lhs, rhs):
    return lax.dot_general(lhs, rhs, (((1,), (1,)), ((), ())), preferred_element_type=F32)


def dot_split(values, rhs):
    rows = values.shape[0]
    both = dot32(jnp.concatenate(split2(values), axis=0), rhs)
    return both[:rows] + both[rows:]


def one_hot(index, depth):
    return (lax.broadcasted_iota(jnp.int32, (depth, index.shape[0]), 0) == index[None, :]).astype(BF16)


def solved_kernel(extra_ref, down_ref):
    width, half = down_ref.shape
    places, sub, lanes = extra_ref.shape
    parts = width // (places * sub)
    at = lanes - (parts + 1) * half
    for place in range(places):
        for b in range(parts):
            row = (place * parts + b) * sub
            down_ref[row : row + sub, :] = extra_ref[place, :, at + b * half : at + (b + 1) * half]


def middle_kernel(
    flag_ref, mine_ref, theirs_ref, head_ref, down_ref, down0_ref, down1_ref, inv_ref, share_ref, own_ref, mix_ref
):
    half_images = mine_ref.shape[0]
    width = head_ref.shape[1]
    images = 2 * half_images
    half = down0_ref.shape[1]
    logits = head_ref.shape[0] // 4
    first_core = flag_ref[1] == 0
    run = width // 2 + half
    mine, theirs = (
        jnp.concatenate([source[:, : width // 2], source[:, run : run + width // 2]], axis=1)
        for source in (mine_ref, theirs_ref)
    )
    for side, source in ((flag_ref[1], mine_ref), (1 - flag_ref[1], theirs_ref)):
        mix_ref[side, :half_images, :] = source[:, width // 2 : run]
        mix_ref[side, half_images:images, :] = source[:, run + width // 2 :]
    block = jnp.concatenate([jnp.where(first_core, mine, theirs), jnp.where(first_core, theirs, mine)], axis=0)
    centred = block - jnp.mean(block, axis=1, keepdims=True)
    inv_std = lax.rsqrt(jnp.mean(centred * centred, axis=1, keepdims=True) + 1e-06)
    xhat = centred * inv_std
    inv_ref[...] = inv_std
    high = xhat.astype(BF16)
    low = (xhat - high.astype(F32)).astype(BF16)
    head = head_ref[...]
    both = jnp.concatenate([high, low], axis=0)
    share = dot_t(both, head[2 * logits :])
    share = share[:images] + share[images:]
    share_ref[...] = (share[:, :logits] + share[:, logits:]) / width
    lhs = jnp.concatenate([both, head[: 2 * logits]], axis=0)

    def write(rhs_ref, put):
        product = dot32(lhs, rhs_ref[...])
        tail = product[2 * images :]
        put(slice(0, images), product[:images] + product[images : 2 * images])
        put(slice(images, images + logits), tail[:logits] + tail[logits:])

    def put_own(rows, values):
        own_ref[rows, :] = values

    def put_mine(rows, values):
        mix_ref[flag_ref[1], images + rows.start : images + rows.stop, :] = values

    def put_theirs(rows, values):
        mix_ref[1 - flag_ref[1], images + rows.start : images + rows.stop, :] = values

    write(down_ref, put_own)
    write(down0_ref, put_mine)
    write(down1_ref, put_theirs)


def last_kernel(flag_ref, gain_ref, inv_ref, share_ref, own_ref, mix_ref, inverse_ref, extra_ref, out_ref):
    images = gain_ref.shape[0]
    logits = share_ref.shape[1]
    panel = inverse_ref.shape[1]
    first_image = pl.multiple_of(pl.program_id(0) * STEP, STEP)
    here = pl.ds(first_image, STEP)
    inv_std = inv_ref[here, :]
    diagonal = lax.broadcasted_iota(jnp.int32, (1, logits, logits), 1) == lax.broadcasted_iota(
        jnp.int32, (1, logits, logits), 2
    )
    share = jnp.sum(jnp.where(diagonal, share_ref[here, :][:, None, :], 0.0), axis=2, keepdims=True)

    def jacobian(gain, along, head):
        scale = gain * inv_std
        values = scale[:, None, :] * (head[None] - share * along[:, None, :])
        return values.reshape(STEP * logits, values.shape[2])

    def solved_side(side):
        along = mix_ref[side, pl.ds(images + first_image, STEP), :]
        return jacobian(mix_ref[side, here, :], along, mix_ref[side, 2 * images : 2 * images + logits, :])

    def inverted(values, inverse):
        high = values.astype(BF16)
        low = (values - high.astype(F32)).astype(BF16)
        return (dot_t(high, inverse) + dot_t(low, inverse)).astype(BF16)

    first = inverted(solved_side(0), inverse_ref[0])
    rows_dev = gain_ref.shape[1]
    panel_01 = extra_ref[:, :, extra_ref.shape[2] - panel :].reshape(panel, panel)
    second = inverted(solved_side(1) - dot32(first, panel_01), inverse_ref[1])
    own = jacobian(gain_ref[here, :], own_ref[here, :], own_ref[images : images + logits, :])
    panel_0 = extra_ref[:, :, :rows_dev].reshape(panel, rows_dev)
    panel_1 = extra_ref[:, :, rows_dev : 2 * rows_dev].reshape(panel, rows_dev)
    below = (own - (dot32(first, panel_0) + dot32(second, panel_1))).astype(BF16)
    out_ref[...] = below.reshape(out_ref.shape)

    @pl.when(flag_ref[0] == 1)
    def _():
        out_ref[:, :, :panel] = first.reshape(STEP, logits, panel)
        out_ref[:, :, panel : 2 * panel] = second.reshape(STEP, logits, panel)


def body(normed, residual_in, w_up, w_down, final_gain, head_cols, sub_inputs, sub_hidden, panels, inverses):
    images, width = normed.shape
    own, hidden_dev = w_up.shape
    logits = head_cols.shape[1]
    panel = inverses.shape[1]
    panel_dev = panels.shape[1]
    rows_dev = sub_inputs.shape[0]
    z_hi, core = lax.axis_index("zh"), lax.axis_index("c")
    rank = z_hi * 2 + core
    local_hidden = sub_hidden - rank * hidden_dev
    half = panel
    vmem = pl.BlockSpec(memory_space=pltpu.VMEM)
    smem = pl.BlockSpec(memory_space=pltpu.SMEM)
    flag = jnp.stack([jnp.where(rank == 0, 1, 0), core, lax.axis_index("zl")]).astype(jnp.int32)

    both = jnp.concatenate([w_up, w_down.T], axis=0)
    line = gather_by_sends(both, "zl", 4)
    line = pl.pallas_call(
        weights_kernel,
        out_shape=jax.ShapeDtypeStruct((16, 8 * own, hidden_dev), BF16),
        in_specs=[vmem],
        out_specs=pl.BlockSpec(memory_space=pltpu.HBM),
        scratch_shapes=[pltpu.VMEM((8 * own, hidden_dev), BF16), pltpu.SemaphoreType.DMA((16,))],
        compiler_params=LARGE,
        name="merge_weights",
    )(line)
    plane = lax.all_to_all(line, ("x", "y"), 0, 0)

    pick_first = one_hot(local_hidden[: 2 * panel], hidden_dev)
    chosen = dot32(both[own:], pick_first).astype(BF16)
    block01 = panels[0][:, panel : 2 * panel]
    chosen = [jnp.concatenate([chosen[:, at : at + half], block01], axis=0) for at in (0, half)]
    payload = jnp.where(core == 0, chosen[0], lax.ppermute(chosen[1], "c", [(0, 1)]))
    payload = jnp.where(z_hi == 1, lax.ppermute(payload, "zh", [(0, 1)]), payload)
    payload = jnp.where(z_hi >= 2, lax.ppermute(payload, "zh", [(0, 3), (1, 2)]), payload)

    chunks = rows_dev // half
    narrow = panels.reshape(2 * panel_dev * chunks, half)
    narrow = jnp.concatenate([narrow, payload], axis=0)
    pieces = ring_pieces(narrow, "zl", 4)
    device, source = [], []
    for q in range(2):
        for b in range(chunks):
            device += [r // panel_dev for r in range(4 * panel_dev)]
            source += [(q * panel_dev + r % panel_dev) * chunks + b for r in range(4 * panel_dev)]
    at = 2 * panel_dev * chunks
    device += [r // own for r in range(4 * own)] + [r // panel_dev for r in range(4 * panel_dev)]
    source += [at + r % own for r in range(4 * own)] + [at + own + r % panel_dev for r in range(4 * panel_dev)]
    extra = pl.pallas_call(
        extra_kernel,
        out_shape=jax.ShapeDtypeStruct((16, 16, len(device) // 16 * half), BF16),
        in_specs=[smem] + [vmem] * 6,
        out_specs=pl.BlockSpec(memory_space=pltpu.HBM),
        scratch_shapes=[pltpu.VMEM((16, len(device) // 16 * half), BF16), pltpu.SemaphoreType.DMA((16,))],
        compiler_params=LARGE,
        name="merge_extra",
    )(flag, np.array(device, np.int32)[:, None], np.array(source, np.int32)[:, None], *pieces)
    extra = lax.all_to_all(extra, ("x", "y"), 0, 0)

    picked = dot32(normed, one_hot(sub_inputs, width))
    kept, given, slope = pl.pallas_call(
        forward_kernel,
        out_shape=(
            jax.ShapeDtypeStruct((images // 2, width + 2 * half), F32),
            jax.ShapeDtypeStruct((images // 2, width + 2 * half), F32),
            jax.ShapeDtypeStruct((images, hidden_dev), F32),
        ),
        in_specs=[smem] + [vmem] * 4,
        out_specs=(vmem,) * 3,
        scratch_shapes=[pltpu.VMEM((images, width), F32)],
        compiler_params=LIMIT,
        name="forward",
    )(flag, normed, plane, local_hidden[None, : 2 * panel], picked)
    pair = kept + swap_core(given)
    run = width // 2 + half
    is_block = lax.broadcasted_iota(jnp.int32, (images // 2, run), 1) < width // 2
    routes = ([(i, i ^ 1) for i in range(4)], [(i, 3 - i) for i in range(4)])
    runs = [pair[:, :run], pair[:, run:]]
    near = [lax.ppermute(part.astype(BF16), "zh", route) for part, route in zip(runs, routes)]
    runs = [
        jnp.where(is_block, part + got.astype(F32), jnp.where(z_hi == first, got.astype(F32), part))
        for part, got, first in zip(runs, near, (1, 3))
    ]
    far = [lax.ppermute(part.astype(BF16), "zh", route) for part, route in zip(runs, routes[::-1])]

    pick_own = one_hot(local_hidden, hidden_dev)
    down_t = plane[:, 4 * own :].reshape(width, hidden_dev)
    down_own = dot32(down_t, pick_own).astype(BF16)
    gain_own = dot_split(slope, pick_own) * picked
    head = final_gain[:, None] * head_cols.astype(F32)
    centred_head = head - jnp.mean(head, axis=0)
    head_parts = jnp.concatenate(split2(centred_head.T) + split2(head.T), axis=0)

    mine = lax.dynamic_slice_in_dim(residual_in, core * (images // 2), images // 2, 0).astype(F32)
    mine = jnp.pad(mine.reshape(images // 2, 2, width // 2), ((0, 0), (0, 0), (0, half)))
    block = jnp.concatenate(
        [
            jnp.where(is_block, mine[:, k] + (runs[k] + far[k].astype(F32)), jnp.where(late, far[k].astype(F32), runs[k]))
            for k, late in enumerate((z_hi >= 2, (z_hi == 1) | (z_hi == 2)))
        ],
        axis=1,
    )
    block_pair = swap_core(block)

    down_mine = pl.pallas_call(
        solved_kernel,
        out_shape=jax.ShapeDtypeStruct((width, half), BF16),
        in_specs=[vmem],
        out_specs=vmem,
        compiler_params=LIMIT,
        name="solved",
    )(extra)
    down_theirs = swap_core(down_mine)
    inv_std, share, own_products, mix = pl.pallas_call(
        middle_kernel,
        out_shape=(
            jax.ShapeDtypeStruct((images, 1), F32),
            jax.ShapeDtypeStruct((images, logits), F32),
            jax.ShapeDtypeStruct((images + logits, rows_dev), F32),
            jax.ShapeDtypeStruct((2, 2 * images + logits, half), F32),
        ),
        in_specs=[smem] + [vmem] * 6,
        out_specs=(vmem,) * 4,
        compiler_params=LIMIT,
        name="middle",
    )(flag, block, block_pair, head_parts, down_own, down_mine, down_theirs)
    return pl.pallas_call(
        last_kernel,
        grid=(images // STEP,),
        out_shape=jax.ShapeDtypeStruct((images, logits, rows_dev), BF16),
        in_specs=[smem] + [vmem] * 7,
        out_specs=pl.BlockSpec((STEP, logits, rows_dev), lambda i: (i, 0, 0)),
        compiler_params=LIMIT,
        name="last",
    )(flag, gain_own, inv_std, share, own_products, mix, inverses, extra)


def solution(mesh):
    fine = Mesh(mesh.devices.reshape(4, 4, 4, 4, 2), ("x", "y", "zl", "zh", "c"))
    in_specs = (
        P(DP, None),
        P(DP, None),
        P(DP, TENSOR),
        P(TENSOR, DP),
        P(),
        P(),
        P(TENSOR),
        P(TENSOR),
        P(None, DP, TENSOR),
        P(),
    )
    out_specs = P(DP, None, TENSOR)

    return jax.shard_map(body, mesh=fine, in_specs=in_specs, out_specs=out_specs, check_vma=False)
```

```python
import jax
import jax.numpy as jnp
import numpy as np
from jax import lax
from jax.experimental import pallas as pl
from jax.experimental.pallas import tpu as pltpu
from jax.sharding import Mesh, PartitionSpec as P

DP = ("x", "y", "zl")
TENSOR = ("zh", "c")
F32 = jnp.float32
BF16 = jnp.bfloat16
STEP = 16
LARGE = pltpu.CompilerParams(vmem_limit_bytes=60 * 1024 * 1024)
LIMIT = pltpu.CompilerParams(vmem_limit_bytes=20 * 1024 * 1024)


def gelu_parts(values):
    normal_cdf = 0.5 * (1.0 + jax.scipy.special.erf(values * 0.7071067811865476))
    slope = normal_cdf + values * jnp.exp(-0.5 * values * values) * 0.3989422804014327
    return (values * normal_cdf, slope)


def swap_core(values):
    return lax.ppermute(values, "c", [(0, 1), (1, 0)])


def gather_by_sends(shard, axis, count):
    spread = jnp.broadcast_to(shard[None], (count,) + shard.shape)
    return lax.all_to_all(spread, axis, 0, 0)


def ring_pieces(shard, axis, count):
    return [shard] + [
        lax.ppermute(shard, axis, [(i, (i - k) % count) for i in range(count)]) for k in range(1, count)
    ]


def weights_kernel(line_ref, out_ref, merged, done):
    pieces, rows, _ = line_ref.shape
    own = rows // 2
    shape = (pieces * rows, rows)
    row, source = (lax.broadcasted_iota(jnp.int32, shape, axis) for axis in (0, 1))
    total = None
    for k in range(pieces):
        target = source + k * own + jnp.where(source < own, 0, (pieces - 1) * own)
        part = dot32((row == target).astype(BF16), line_ref[k])
        total = part if total is None else total + part
    merged[...] = total.astype(BF16)
    send_copies(merged, out_ref, done)


def send_copies(merged, out_ref, done):
    copies = [pltpu.make_async_copy(merged, out_ref.at[place], done.at[place]) for place in range(out_ref.shape[0])]
    for copy in copies:
        copy.start()
    for copy in copies:
        copy.wait()


def extra_kernel(flag_ref, device_ref, row_ref, p0, p1, p2, p3, out_ref, merged, done):
    sub = merged.shape[0]
    rows, half = p0.shape
    code = jnp.bitwise_and(device_ref[...] - flag_ref[2], 3) * rows + row_ref[...]
    total = None
    for k, piece in enumerate((p0, p1, p2, p3)):
        lane = lax.broadcasted_iota(jnp.int32, (code.shape[0], rows), 1) + k * rows
        part = dot32((lane == code).astype(BF16), piece[...])
        total = part if total is None else total + part
    line = total.astype(BF16)
    for b in range(line.shape[0] // sub):
        merged[:, b * half : (b + 1) * half] = line[b * sub : (b + 1) * sub, :]
    send_copies(merged, out_ref, done)


def forward_kernel(flag_ref, normed_ref, plane_ref, index_ref, picked_ref, kept_ref, given_ref, slope_ref, part):
    _, rows, hidden_dev = plane_ref.shape
    images, width = normed_ref.shape
    half_images = kept_ref.shape[0]
    solved = index_ref.shape[1]
    half = solved // 2
    up_pre = dot32(normed_ref[...], plane_ref[:, : rows // 2, :].reshape(width, hidden_dev))
    activ, slope = gelu_parts(up_pre)
    slope_ref[...] = slope
    down_t = plane_ref[:, rows // 2 :, :].reshape(width, hidden_dev)
    part[...] = dot_t(activ.astype(BF16), down_t)
    core = flag_ref[1]
    high = slope.astype(BF16)
    low = (slope - high.astype(F32)).astype(BF16)
    pick = (lax.broadcasted_iota(jnp.int32, (hidden_dev, solved), 0) == index_ref[...]).astype(BF16)
    gain = dot32(jnp.concatenate([high, low], axis=0), pick)
    gain = jnp.where(core == 0, (gain[:images] + gain[images:]) * picked_ref[:, :solved], 0.0)
    for out, side, at in ((kept_ref, core, 0), (given_ref, 1 - core, half)):
        rows_here = pl.ds(pl.multiple_of(side * half_images, half_images), half_images)
        for run in range(2):
            base = run * (width // 2 + half)
            out[:, base : base + width // 2] = part[rows_here, run * (width // 2) : (run + 1) * (width // 2)]
            out[:, base + width // 2 : base + width // 2 + half] = gain[
                run * half_images : (run + 1) * half_images, at : at + half
            ]


def split2(values):
    high = lax.reduce_precision(values, 8, 7)
    return high.astype(BF16), (values - high).astype(BF16)


def dot32(lhs, rhs):
    return jnp.dot(lhs, rhs, preferred_element_type=F32)


def dot_t(lhs, rhs):
    return lax.dot_general(lhs, rhs, (((1,), (1,)), ((), ())), preferred_element_type=F32)


def dot_split(values, rhs):
    rows = values.shape[0]
    both = dot32(jnp.concatenate(split2(values), axis=0), rhs)
    return both[:rows] + both[rows:]


def one_hot(index, depth):
    return (lax.broadcasted_iota(jnp.int32, (depth, index.shape[0]), 0) == index[None, :]).astype(BF16)


def solved_kernel(extra_ref, down_ref):
    width, half = down_ref.shape
    places, sub, lanes = extra_ref.shape
    parts = width // (places * sub)
    at = lanes - (parts + 1) * half
    for place in range(places):
        for b in range(parts):
            row = (place * parts + b) * sub
            down_ref[row : row + sub, :] = extra_ref[place, :, at + b * half : at + (b + 1) * half]


def middle_kernel(
    flag_ref, mine_ref, theirs_ref, head_ref, down_ref, down0_ref, down1_ref, inv_ref, share_ref, own_ref, mix_ref
):
    half_images = mine_ref.shape[0]
    width = head_ref.shape[1]
    images = 2 * half_images
    half = down0_ref.shape[1]
    logits = head_ref.shape[0] // 4
    first_core = flag_ref[1] == 0
    run = width // 2 + half
    mine, theirs = (
        jnp.concatenate([source[:, : width // 2], source[:, run : run + width // 2]], axis=1)
        for source in (mine_ref, theirs_ref)
    )
    for side, source in ((flag_ref[1], mine_ref), (1 - flag_ref[1], theirs_ref)):
        mix_ref[side, :half_images, :] = source[:, width // 2 : run]
        mix_ref[side, half_images:images, :] = source[:, run + width // 2 :]
    block = jnp.concatenate([jnp.where(first_core, mine, theirs), jnp.where(first_core, theirs, mine)], axis=0)
    centred = block - jnp.mean(block, axis=1, keepdims=True)
    inv_std = lax.rsqrt(jnp.mean(centred * centred, axis=1, keepdims=True) + 1e-06)
    xhat = centred * inv_std
    inv_ref[...] = inv_std
    high = xhat.astype(BF16)
    low = (xhat - high.astype(F32)).astype(BF16)
    head = head_ref[...]
    both = jnp.concatenate([high, low], axis=0)
    share = dot_t(both, head[2 * logits :])
    share = share[:images] + share[images:]
    share_ref[...] = (share[:, :logits] + share[:, logits:]) / width
    lhs = jnp.concatenate([both, head[: 2 * logits]], axis=0)

    def write(rhs_ref, put):
        product = dot32(lhs, rhs_ref[...])
        tail = product[2 * images :]
        put(slice(0, images), product[:images] + product[images : 2 * images])
        put(slice(images, images + logits), tail[:logits] + tail[logits:])

    def put_own(rows, values):
        own_ref[rows, :] = values

    def put_mine(rows, values):
        mix_ref[flag_ref[1], images + rows.start : images + rows.stop, :] = values

    def put_theirs(rows, values):
        mix_ref[1 - flag_ref[1], images + rows.start : images + rows.stop, :] = values

    write(down_ref, put_own)
    write(down0_ref, put_mine)
    write(down1_ref, put_theirs)


def last_kernel(
    flag_ref, gain_ref, inv_ref, share_ref, own_ref, mix_ref, inverse_ref, extra_ref, out_ref, result, done
):
    images, rows_dev = gain_ref.shape
    logits = share_ref.shape[1]
    panel = inverse_ref.shape[1]
    diagonal = lax.broadcasted_iota(jnp.int32, (1, logits, logits), 1) == lax.broadcasted_iota(
        jnp.int32, (1, logits, logits), 2
    )
    panel_01 = extra_ref[:, :, extra_ref.shape[2] - panel :].reshape(panel, panel)
    panel_0 = extra_ref[:, :, :rows_dev].reshape(panel, rows_dev)
    panel_1 = extra_ref[:, :, rows_dev : 2 * rows_dev].reshape(panel, rows_dev)

    def inverted(values, inverse):
        high = values.astype(BF16)
        low = (values - high.astype(F32)).astype(BF16)
        return (dot_t(high, inverse) + dot_t(low, inverse)).astype(BF16)

    copies = []
    for step in range(images // STEP):
        here = slice(step * STEP, (step + 1) * STEP)
        inv_std = inv_ref[here, :]
        share = jnp.sum(jnp.where(diagonal, share_ref[here, :][:, None, :], 0.0), axis=2, keepdims=True)

        def jacobian(gain, along, head):
            scale = gain * inv_std
            values = scale[:, None, :] * (head[None] - share * along[:, None, :])
            return values.reshape(STEP * logits, values.shape[2])

        def solved_side(side):
            along = mix_ref[side, images + step * STEP : images + (step + 1) * STEP, :]
            return jacobian(mix_ref[side, here, :], along, mix_ref[side, 2 * images : 2 * images + logits, :])

        first = inverted(solved_side(0), inverse_ref[0])
        second = inverted(solved_side(1) - dot32(first, panel_01), inverse_ref[1])
        own = jacobian(gain_ref[here, :], own_ref[here, :], own_ref[images : images + logits, :])
        below = (own - (dot32(first, panel_0) + dot32(second, panel_1))).astype(BF16)
        holder = flag_ref[0] == 1
        top = below[:, : 2 * panel]
        top = jnp.where(holder, jnp.concatenate([first, second], axis=1), top)
        result[here, :, : 2 * panel] = top.reshape(STEP, logits, 2 * panel)
        result[here, :, 2 * panel :] = below[:, 2 * panel :].reshape(STEP, logits, rows_dev - 2 * panel)
        copies.append(pltpu.make_async_copy(result.at[here], out_ref.at[here], done.at[step]))
        copies[-1].start()
    for copy in copies:
        copy.wait()


def body(normed, residual_in, w_up, w_down, final_gain, head_cols, sub_inputs, sub_hidden, panels, inverses):
    images, width = normed.shape
    own, hidden_dev = w_up.shape
    logits = head_cols.shape[1]
    panel = inverses.shape[1]
    panel_dev = panels.shape[1]
    rows_dev = sub_inputs.shape[0]
    z_hi, core = lax.axis_index("zh"), lax.axis_index("c")
    rank = z_hi * 2 + core
    local_hidden = sub_hidden - rank * hidden_dev
    half = panel
    vmem = pl.BlockSpec(memory_space=pltpu.VMEM)
    smem = pl.BlockSpec(memory_space=pltpu.SMEM)
    flag = jnp.stack([jnp.where(rank == 0, 1, 0), core, lax.axis_index("zl")]).astype(jnp.int32)

    both = jnp.concatenate([w_up, w_down.T], axis=0)
    line = gather_by_sends(both, "zl", 4)
    line = pl.pallas_call(
        weights_kernel,
        out_shape=jax.ShapeDtypeStruct((16, 8 * own, hidden_dev), BF16),
        in_specs=[vmem],
        out_specs=pl.BlockSpec(memory_space=pltpu.HBM),
        scratch_shapes=[pltpu.VMEM((8 * own, hidden_dev), BF16), pltpu.SemaphoreType.DMA((16,))],
        compiler_params=LARGE,
        name="merge_weights",
    )(line)
    plane = lax.all_to_all(line, ("x", "y"), 0, 0)

    pick_first = one_hot(local_hidden[: 2 * panel], hidden_dev)
    chosen = dot32(both[own:], pick_first).astype(BF16)
    block01 = panels[0][:, panel : 2 * panel]
    chosen = [jnp.concatenate([chosen[:, at : at + half], block01], axis=0) for at in (0, half)]
    payload = jnp.where(core == 0, chosen[0], lax.ppermute(chosen[1], "c", [(0, 1)]))
    payload = jnp.where(z_hi == 1, lax.ppermute(payload, "zh", [(0, 1)]), payload)
    payload = jnp.where(z_hi >= 2, lax.ppermute(payload, "zh", [(0, 3), (1, 2)]), payload)

    chunks = rows_dev // half
    narrow = panels.reshape(2 * panel_dev * chunks, half)
    narrow = jnp.concatenate([narrow, payload], axis=0)
    pieces = ring_pieces(narrow, "zl", 4)
    device, source = [], []
    for q in range(2):
        for b in range(chunks):
            device += [r // panel_dev for r in range(4 * panel_dev)]
            source += [(q * panel_dev + r % panel_dev) * chunks + b for r in range(4 * panel_dev)]
    at = 2 * panel_dev * chunks
    device += [r // own for r in range(4 * own)] + [r // panel_dev for r in range(4 * panel_dev)]
    source += [at + r % own for r in range(4 * own)] + [at + own + r % panel_dev for r in range(4 * panel_dev)]
    extra = pl.pallas_call(
        extra_kernel,
        out_shape=jax.ShapeDtypeStruct((16, 16, len(device) // 16 * half), BF16),
        in_specs=[smem] + [vmem] * 6,
        out_specs=pl.BlockSpec(memory_space=pltpu.HBM),
        scratch_shapes=[pltpu.VMEM((16, len(device) // 16 * half), BF16), pltpu.SemaphoreType.DMA((16,))],
        compiler_params=LARGE,
        name="merge_extra",
    )(flag, np.array(device, np.int32)[:, None], np.array(source, np.int32)[:, None], *pieces)
    extra = lax.all_to_all(extra, ("x", "y"), 0, 0)

    picked = dot32(normed, one_hot(sub_inputs, width))
    kept, given, slope = pl.pallas_call(
        forward_kernel,
        out_shape=(
            jax.ShapeDtypeStruct((images // 2, width + 2 * half), F32),
            jax.ShapeDtypeStruct((images // 2, width + 2 * half), F32),
            jax.ShapeDtypeStruct((images, hidden_dev), F32),
        ),
        in_specs=[smem] + [vmem] * 4,
        out_specs=(vmem,) * 3,
        scratch_shapes=[pltpu.VMEM((images, width), F32)],
        compiler_params=LIMIT,
        name="forward",
    )(flag, normed, plane, local_hidden[None, : 2 * panel], picked)
    pair = kept + swap_core(given)
    run = width // 2 + half
    is_block = lax.broadcasted_iota(jnp.int32, (images // 2, run), 1) < width // 2
    routes = ([(i, i ^ 1) for i in range(4)], [(i, 3 - i) for i in range(4)])
    runs = [pair[:, :run], pair[:, run:]]
    near = [lax.ppermute(part.astype(BF16), "zh", route) for part, route in zip(runs, routes)]
    runs = [
        jnp.where(is_block, part + got.astype(F32), jnp.where(z_hi == first, got.astype(F32), part))
        for part, got, first in zip(runs, near, (1, 3))
    ]
    far = [lax.ppermute(part.astype(BF16), "zh", route) for part, route in zip(runs, routes[::-1])]

    pick_own = one_hot(local_hidden, hidden_dev)
    down_t = plane[:, 4 * own :].reshape(width, hidden_dev)
    down_own = dot32(down_t, pick_own).astype(BF16)
    gain_own = dot_split(slope, pick_own) * picked
    head = final_gain[:, None] * head_cols.astype(F32)
    centred_head = head - jnp.mean(head, axis=0)
    head_parts = jnp.concatenate(split2(centred_head.T) + split2(head.T), axis=0)

    mine = lax.dynamic_slice_in_dim(residual_in, core * (images // 2), images // 2, 0).astype(F32)
    mine = jnp.pad(mine.reshape(images // 2, 2, width // 2), ((0, 0), (0, 0), (0, half)))
    block = jnp.concatenate(
        [
            jnp.where(is_block, mine[:, k] + (runs[k] + far[k].astype(F32)), jnp.where(late, far[k].astype(F32), runs[k]))
            for k, late in enumerate((z_hi >= 2, (z_hi == 1) | (z_hi == 2)))
        ],
        axis=1,
    )
    block_pair = swap_core(block)

    down_mine = pl.pallas_call(
        solved_kernel,
        out_shape=jax.ShapeDtypeStruct((width, half), BF16),
        in_specs=[vmem],
        out_specs=vmem,
        compiler_params=LIMIT,
        name="solved",
    )(extra)
    down_theirs = swap_core(down_mine)
    inv_std, share, own_products, mix = pl.pallas_call(
        middle_kernel,
        out_shape=(
            jax.ShapeDtypeStruct((images, 1), F32),
            jax.ShapeDtypeStruct((images, logits), F32),
            jax.ShapeDtypeStruct((images + logits, rows_dev), F32),
            jax.ShapeDtypeStruct((2, 2 * images + logits, half), F32),
        ),
        in_specs=[smem] + [vmem] * 6,
        out_specs=(vmem,) * 4,
        compiler_params=LIMIT,
        name="middle",
    )(flag, block, block_pair, head_parts, down_own, down_mine, down_theirs)
    return pl.pallas_call(
        last_kernel,
        out_shape=jax.ShapeDtypeStruct((images, logits, rows_dev), BF16),
        in_specs=[smem] + [vmem] * 7,
        out_specs=pl.BlockSpec(memory_space=pltpu.HBM),
        scratch_shapes=[
            pltpu.VMEM((images, logits, rows_dev), BF16),
            pltpu.SemaphoreType.DMA((images // STEP,)),
        ],
        compiler_params=LIMIT,
        name="last",
    )(flag, gain_own, inv_std, share, own_products, mix, inverses, extra)


def solution(mesh):
    fine = Mesh(mesh.devices.reshape(4, 4, 4, 4, 2), ("x", "y", "zl", "zh", "c"))
    in_specs = (
        P(DP, None),
        P(DP, None),
        P(DP, TENSOR),
        P(TENSOR, DP),
        P(),
        P(),
        P(TENSOR),
        P(TENSOR),
        P(None, DP, TENSOR),
        P(),
    )
    out_specs = P(DP, None, TENSOR)

    return jax.shard_map(body, mesh=fine, in_specs=in_specs, out_specs=out_specs, check_vma=False)
```

```python
import jax
import jax.numpy as jnp
import numpy as np
from jax import lax
from jax.experimental import pallas as pl
from jax.experimental.pallas import tpu as pltpu
from jax.sharding import Mesh, PartitionSpec as P

DP = ("x", "y", "zl")
TENSOR = ("zh", "c")
F32 = jnp.float32
BF16 = jnp.bfloat16
STEP = 32
LARGE = pltpu.CompilerParams(vmem_limit_bytes=60 * 1024 * 1024)
LIMIT = pltpu.CompilerParams(vmem_limit_bytes=20 * 1024 * 1024)


def gelu_parts(values):
    normal_cdf = 0.5 * (1.0 + jax.scipy.special.erf(values * 0.7071067811865476))
    slope = normal_cdf + values * jnp.exp(-0.5 * values * values) * 0.3989422804014327
    return (values * normal_cdf, slope)


def swap_core(values):
    return lax.ppermute(values, "c", [(0, 1), (1, 0)])


def gather_by_sends(shard, axis, count):
    spread = jnp.broadcast_to(shard[None], (count,) + shard.shape)
    return lax.all_to_all(spread, axis, 0, 0)


def ring_pieces(shard, axis, count):
    return [shard] + [
        lax.ppermute(shard, axis, [(i, (i - k) % count) for i in range(count)]) for k in range(1, count)
    ]


def weights_kernel(line_ref, out_ref):
    pieces, rows, _ = line_ref.shape
    own = rows // 2
    shape = (pieces * rows, rows)
    row, source = (lax.broadcasted_iota(jnp.int32, shape, axis) for axis in (0, 1))
    total = None
    for k in range(pieces):
        target = source + k * own + jnp.where(source < own, 0, (pieces - 1) * own)
        part = dot32((row == target).astype(BF16), line_ref[k])
        total = part if total is None else total + part
    line = total.astype(BF16)
    for place in range(out_ref.shape[0]):
        out_ref[place] = line


def send_copies(merged, out_ref, done):
    copies = [pltpu.make_async_copy(merged, out_ref.at[place], done.at[place]) for place in range(out_ref.shape[0])]
    for copy in copies:
        copy.start()
    for copy in copies:
        copy.wait()


def extra_kernel(flag_ref, device_ref, row_ref, p0, p1, p2, p3, out_ref, merged, done):
    sub = merged.shape[0]
    rows, half = p0.shape
    code = jnp.bitwise_and(device_ref[...] - flag_ref[2], 3) * rows + row_ref[...]
    total = None
    for k, piece in enumerate((p0, p1, p2, p3)):
        lane = lax.broadcasted_iota(jnp.int32, (code.shape[0], rows), 1) + k * rows
        part = dot32((lane == code).astype(BF16), piece[...])
        total = part if total is None else total + part
    line = total.astype(BF16)
    for b in range(line.shape[0] // sub):
        merged[:, b * half : (b + 1) * half] = line[b * sub : (b + 1) * sub, :]
    send_copies(merged, out_ref, done)


def forward_kernel(flag_ref, normed_ref, plane_ref, index_ref, picked_ref, kept_ref, given_ref, slope_ref, part):
    _, rows, hidden_dev = plane_ref.shape
    images, width = normed_ref.shape
    half_images = kept_ref.shape[0]
    solved = index_ref.shape[1]
    half = solved // 2
    up_pre = dot32(normed_ref[...], plane_ref[:, : rows // 2, :].reshape(width, hidden_dev))
    activ, slope = gelu_parts(up_pre)
    slope_ref[...] = slope
    down_t = plane_ref[:, rows // 2 :, :].reshape(width, hidden_dev)
    part[...] = dot_t(activ.astype(BF16), down_t)
    core = flag_ref[1]
    high = slope.astype(BF16)
    low = (slope - high.astype(F32)).astype(BF16)
    pick = (lax.broadcasted_iota(jnp.int32, (hidden_dev, solved), 0) == index_ref[...]).astype(BF16)
    gain = dot32(jnp.concatenate([high, low], axis=0), pick)
    gain = jnp.where(core == 0, (gain[:images] + gain[images:]) * picked_ref[:, :solved], 0.0)
    for out, side, at in ((kept_ref, core, 0), (given_ref, 1 - core, half)):
        rows_here = pl.ds(pl.multiple_of(side * half_images, half_images), half_images)
        out[:, :width] = part[rows_here, :]
        out[:, width : width + half] = gain[:half_images, at : at + half]
        out[:, width + half :] = gain[half_images:, at : at + half]


def split2(values):
    high = lax.reduce_precision(values, 8, 7)
    return high.astype(BF16), (values - high).astype(BF16)


def dot32(lhs, rhs):
    return jnp.dot(lhs, rhs, preferred_element_type=F32)


def dot_t(lhs, rhs):
    return lax.dot_general(lhs, rhs, (((1,), (1,)), ((), ())), preferred_element_type=F32)


def dot_split(values, rhs):
    rows = values.shape[0]
    both = dot32(jnp.concatenate(split2(values), axis=0), rhs)
    return both[:rows] + both[rows:]


def one_hot(index, depth):
    return (lax.broadcasted_iota(jnp.int32, (depth, index.shape[0]), 0) == index[None, :]).astype(BF16)


def solved_kernel(extra_ref, down_ref):
    width, half = down_ref.shape
    places, sub, lanes = extra_ref.shape
    parts = width // (places * sub)
    at = lanes - (parts + 1) * half
    for place in range(places):
        for b in range(parts):
            row = (place * parts + b) * sub
            down_ref[row : row + sub, :] = extra_ref[place, :, at + b * half : at + (b + 1) * half]


def middle_kernel(
    flag_ref, mine_ref, theirs_ref, head_ref, down_ref, down0_ref, down1_ref, inv_ref, share_ref, own_ref, mix_ref
):
    half_images = mine_ref.shape[0]
    width = head_ref.shape[1]
    images = 2 * half_images
    logits = head_ref.shape[0] // 4
    first_core = flag_ref[1] == 0
    mine, theirs = mine_ref[...], theirs_ref[...]
    block = jnp.concatenate([jnp.where(first_core, mine, theirs), jnp.where(first_core, theirs, mine)], axis=0)
    centred = block - jnp.mean(block, axis=1, keepdims=True)
    inv_std = lax.rsqrt(jnp.mean(centred * centred, axis=1, keepdims=True) + 1e-06)
    xhat = centred * inv_std
    inv_ref[...] = inv_std
    high = xhat.astype(BF16)
    low = (xhat - high.astype(F32)).astype(BF16)
    head = head_ref[...]
    both = jnp.concatenate([high, low], axis=0)
    share = dot_t(both, head[2 * logits :])
    share = share[:images] + share[images:]
    share_ref[...] = (share[:, :logits] + share[:, logits:]) / width
    lhs = jnp.concatenate([both, head[: 2 * logits]], axis=0)

    def write(rhs_ref, put):
        product = dot32(lhs, rhs_ref[...])
        tail = product[2 * images :]
        put(slice(0, images), product[:images] + product[images : 2 * images])
        put(slice(images, images + logits), tail[:logits] + tail[logits:])

    def put_own(rows, values):
        own_ref[rows, :] = values

    def put_mine(rows, values):
        mix_ref[flag_ref[1], rows, :] = values

    def put_theirs(rows, values):
        mix_ref[1 - flag_ref[1], rows, :] = values

    write(down_ref, put_own)
    write(down0_ref, put_mine)
    write(down1_ref, put_theirs)


def last_kernel(flag_ref, gain_ref, inv_ref, share_ref, own_ref, mix_ref, mine_ref, theirs_ref, inverse_ref, extra_ref, out_ref):
    images = gain_ref.shape[0]
    logits = share_ref.shape[1]
    panel = inverse_ref.shape[1]
    first_image = pl.multiple_of(pl.program_id(0) * STEP, STEP)
    here = pl.ds(first_image, STEP)
    inv_std = inv_ref[here, :]
    diagonal = lax.broadcasted_iota(jnp.int32, (1, logits, logits), 1) == lax.broadcasted_iota(
        jnp.int32, (1, logits, logits), 2
    )
    share = jnp.sum(jnp.where(diagonal, share_ref[here, :][:, None, :], 0.0), axis=2, keepdims=True)

    def jacobian(gain, along, head):
        scale = gain * inv_std
        values = scale[:, None, :] * head[None] - share * (scale * along)[:, None, :]
        return values.reshape(STEP * logits, values.shape[2])

    def solved_side(side):
        lanes = pl.ds(pl.multiple_of(pl.program_id(0) * panel, panel), panel)
        gain = jnp.where(flag_ref[1] == side, mine_ref[:, lanes], theirs_ref[:, lanes])
        return jacobian(gain, mix_ref[side, here, :], mix_ref[side, images : images + logits, :])

    def inverted(values, inverse):
        return dot_t(values.astype(BF16), inverse).astype(BF16)

    first = inverted(solved_side(0), inverse_ref[0])
    rows_dev = gain_ref.shape[1]
    panel_01 = extra_ref[:, :, extra_ref.shape[2] - panel :].reshape(panel, panel)
    second = inverted(solved_side(1) - dot32(first, panel_01), inverse_ref[1])
    own = jacobian(gain_ref[here, :], own_ref[here, :], own_ref[images : images + logits, :])
    panel_0 = extra_ref[:, :, :rows_dev].reshape(panel, rows_dev)
    panel_1 = extra_ref[:, :, rows_dev : 2 * rows_dev].reshape(panel, rows_dev)
    below = (own - (dot32(first, panel_0) + dot32(second, panel_1))).astype(BF16)
    out_ref[...] = below.reshape(out_ref.shape)

    @pl.when(flag_ref[0] == 1)
    def _():
        out_ref[:, :, :panel] = first.reshape(STEP, logits, panel)
        out_ref[:, :, panel : 2 * panel] = second.reshape(STEP, logits, panel)


def body(normed, residual_in, w_up, w_down, final_gain, head_cols, sub_inputs, sub_hidden, panels, inverses):
    images, width = normed.shape
    own, hidden_dev = w_up.shape
    logits = head_cols.shape[1]
    panel = inverses.shape[1]
    panel_dev = panels.shape[1]
    rows_dev = sub_inputs.shape[0]
    z_hi, core = lax.axis_index("zh"), lax.axis_index("c")
    rank = z_hi * 2 + core
    local_hidden = sub_hidden - rank * hidden_dev
    half = panel
    vmem = pl.BlockSpec(memory_space=pltpu.VMEM)
    smem = pl.BlockSpec(memory_space=pltpu.SMEM)
    flag = jnp.stack([jnp.where(rank == 0, 1, 0), core, lax.axis_index("zl")]).astype(jnp.int32)

    both = jnp.concatenate([w_up, w_down.T], axis=0)
    line = gather_by_sends(both, "zl", 4)
    line = pl.pallas_call(
        weights_kernel,
        out_shape=jax.ShapeDtypeStruct((16, 8 * own, hidden_dev), BF16),
        in_specs=[vmem],
        out_specs=vmem,
        compiler_params=LIMIT,
        name="merge_weights",
    )(line)
    plane = lax.all_to_all(line, ("x", "y"), 0, 0)

    pick_first = one_hot(local_hidden[: 2 * panel], hidden_dev)
    chosen = dot32(both[own:], pick_first).astype(BF16)
    block01 = panels[0][:, panel : 2 * panel]
    chosen = [jnp.concatenate([chosen[:, at : at + half], block01], axis=0) for at in (0, half)]
    payload = jnp.where(core == 0, chosen[0], lax.ppermute(chosen[1], "c", [(0, 1)]))
    payload = jnp.where(z_hi == 1, lax.ppermute(payload, "zh", [(0, 1)]), payload)
    payload = jnp.where(z_hi >= 2, lax.ppermute(payload, "zh", [(0, 3), (1, 2)]), payload)

    chunks = rows_dev // half
    narrow = panels.reshape(2 * panel_dev * chunks, half)
    narrow = jnp.concatenate([narrow, payload], axis=0)
    pieces = ring_pieces(narrow, "zl", 4)
    device, source = [], []
    for q in range(2):
        for b in range(chunks):
            device += [r // panel_dev for r in range(4 * panel_dev)]
            source += [(q * panel_dev + r % panel_dev) * chunks + b for r in range(4 * panel_dev)]
    at = 2 * panel_dev * chunks
    device += [r // own for r in range(4 * own)] + [r // panel_dev for r in range(4 * panel_dev)]
    source += [at + r % own for r in range(4 * own)] + [at + own + r % panel_dev for r in range(4 * panel_dev)]
    extra = pl.pallas_call(
        extra_kernel,
        out_shape=jax.ShapeDtypeStruct((16, 16, len(device) // 16 * half), BF16),
        in_specs=[smem] + [vmem] * 6,
        out_specs=pl.BlockSpec(memory_space=pltpu.HBM),
        scratch_shapes=[pltpu.VMEM((16, len(device) // 16 * half), BF16), pltpu.SemaphoreType.DMA((16,))],
        compiler_params=LARGE,
        name="merge_extra",
    )(flag, np.array(device, np.int32)[:, None], np.array(source, np.int32)[:, None], *pieces)
    extra = lax.all_to_all(extra, ("x", "y"), 0, 0)

    mine = jnp.where(core == 0, residual_in[: images // 2], residual_in[images // 2 :]).astype(F32)
    third = jnp.where(z_hi == 3, 1.0, 0.0) + jnp.zeros((images // 2, 2 * half), F32)
    inner = jnp.where((z_hi == 1) | (z_hi == 2), 1.0, 0.0) + jnp.zeros((images // 2, 2 * half), F32)
    mine, third, inner = lax.optimization_barrier((mine, third, inner))

    picked = dot32(normed, one_hot(sub_inputs, width))
    kept, given, slope = pl.pallas_call(
        forward_kernel,
        out_shape=(
            jax.ShapeDtypeStruct((images // 2, width + 2 * half), F32),
            jax.ShapeDtypeStruct((images // 2, width + 2 * half), F32),
            jax.ShapeDtypeStruct((images, hidden_dev), F32),
        ),
        in_specs=[smem] + [vmem] * 4,
        out_specs=(vmem,) * 3,
        scratch_shapes=[pltpu.VMEM((images, width), F32)],
        compiler_params=LIMIT,
        name="forward",
    )(flag, normed, plane, local_hidden[None, : 2 * panel], picked)
    pair = kept + swap_core(given)
    gain, pair = pair[:, width:], pair[:, :width]
    near = lax.ppermute(pair.astype(BF16), "zh", [(i, i ^ 1) for i in range(4)]).astype(F32)
    got = lax.ppermute(gain.astype(BF16), "zh", [(0, 3)]).astype(F32)
    pair = pair + near
    gain = jnp.where(third > 0.5, got, gain)
    far = lax.ppermute(pair.astype(BF16), "zh", [(i, 3 - i) for i in range(4)]).astype(F32)
    got = lax.ppermute(gain.astype(BF16), "zh", [(0, 1), (3, 2)]).astype(F32)
    gain = jnp.where(inner > 0.5, got, gain)

    pick_own = one_hot(local_hidden, hidden_dev)
    down_t = plane[:, 4 * own :].reshape(width, hidden_dev)
    down_own = dot32(down_t, pick_own).astype(BF16)
    gain_own = dot_split(slope, pick_own) * picked
    head = final_gain[:, None] * head_cols.astype(F32)
    centred_head = head - jnp.mean(head, axis=0)
    head_parts = jnp.concatenate(split2(centred_head.T) + split2(head.T), axis=0)

    block = mine + (pair + far)
    block_pair = swap_core(block)
    gain_pair = swap_core(gain)

    down_mine = pl.pallas_call(
        solved_kernel,
        out_shape=jax.ShapeDtypeStruct((width, half), BF16),
        in_specs=[vmem],
        out_specs=vmem,
        compiler_params=LIMIT,
        name="solved",
    )(extra)
    down_theirs = swap_core(down_mine)
    inv_std, share, own_products, mix = pl.pallas_call(
        middle_kernel,
        out_shape=(
            jax.ShapeDtypeStruct((images, 1), F32),
            jax.ShapeDtypeStruct((images, logits), F32),
            jax.ShapeDtypeStruct((images + logits, rows_dev), F32),
            jax.ShapeDtypeStruct((2, images + logits, half), F32),
        ),
        in_specs=[smem] + [vmem] * 6,
        out_specs=(vmem,) * 4,
        compiler_params=LIMIT,
        name="middle",
    )(flag, block, block_pair, head_parts, down_own, down_mine, down_theirs)
    return pl.pallas_call(
        last_kernel,
        grid=(images // STEP,),
        out_shape=jax.ShapeDtypeStruct((images, logits, rows_dev), BF16),
        in_specs=[smem] + [vmem] * 9,
        out_specs=pl.BlockSpec((STEP, logits, rows_dev), lambda i: (i, 0, 0)),
        compiler_params=LIMIT,
        name="last",
    )(flag, gain_own, inv_std, share, own_products, mix, gain, gain_pair, inverses, extra)


def solution(mesh):
    fine = Mesh(mesh.devices.reshape(4, 4, 4, 4, 2), ("x", "y", "zl", "zh", "c"))
    in_specs = (
        P(DP, None),
        P(DP, None),
        P(DP, TENSOR),
        P(TENSOR, DP),
        P(),
        P(),
        P(TENSOR),
        P(TENSOR),
        P(None, DP, TENSOR),
        P(),
    )
    out_specs = P(DP, None, TENSOR)

    return jax.shard_map(body, mesh=fine, in_specs=in_specs, out_specs=out_specs, check_vma=False)
```

```python
import jax
import jax.numpy as jnp
import numpy as np
from jax import lax
from jax.experimental import pallas as pl
from jax.experimental.pallas import tpu as pltpu
from jax.sharding import Mesh, PartitionSpec as P

DP = ("x", "y", "zl")
TENSOR = ("zh", "c")
F32 = jnp.float32
BF16 = jnp.bfloat16
STEP = 32
LARGE = pltpu.CompilerParams(vmem_limit_bytes=60 * 1024 * 1024)
LIMIT = pltpu.CompilerParams(vmem_limit_bytes=20 * 1024 * 1024)


def gelu_parts(values):
    normal_cdf = 0.5 * (1.0 + jax.scipy.special.erf(values * 0.7071067811865476))
    slope = normal_cdf + values * jnp.exp(-0.5 * values * values) * 0.3989422804014327
    return (values * normal_cdf, slope)


def swap_core(values):
    return lax.ppermute(values, "c", [(0, 1), (1, 0)])


def gather_by_sends(shard, axis, count):
    spread = jnp.broadcast_to(shard[None], (count,) + shard.shape)
    return lax.all_to_all(spread, axis, 0, 0)


def ring_pieces(shard, axis, count):
    return [shard] + [
        lax.ppermute(shard, axis, [(i, (i - k) % count) for i in range(count)]) for k in range(1, count)
    ]


def weights_kernel(line_ref, out_ref):
    pieces, rows, _ = line_ref.shape
    own = rows // 2
    shape = (pieces * rows, rows)
    row, source = (lax.broadcasted_iota(jnp.int32, shape, axis) for axis in (0, 1))
    total = None
    for k in range(pieces):
        target = source + k * own + jnp.where(source < own, 0, (pieces - 1) * own)
        part = dot32((row == target).astype(BF16), line_ref[k])
        total = part if total is None else total + part
    line = total.astype(BF16)
    for place in range(out_ref.shape[0]):
        out_ref[place] = line


def send_copies(merged, out_ref, done):
    copies = [pltpu.make_async_copy(merged, out_ref.at[place], done.at[place]) for place in range(out_ref.shape[0])]
    for copy in copies:
        copy.start()
    for copy in copies:
        copy.wait()


def extra_kernel(flag_ref, device_ref, row_ref, p0, p1, p2, p3, out_ref, merged, done):
    sub = merged.shape[0]
    rows, half = p0.shape
    code = jnp.bitwise_and(device_ref[...] - flag_ref[2], 3) * rows + row_ref[...]
    total = None
    for k, piece in enumerate((p0, p1, p2, p3)):
        lane = lax.broadcasted_iota(jnp.int32, (code.shape[0], rows), 1) + k * rows
        part = dot32((lane == code).astype(BF16), piece[...])
        total = part if total is None else total + part
    line = total.astype(BF16)
    for b in range(line.shape[0] // sub):
        merged[:, b * half : (b + 1) * half] = line[b * sub : (b + 1) * sub, :]
    send_copies(merged, out_ref, done)


def forward_kernel(flag_ref, normed_ref, plane_ref, index_ref, picked_ref, kept_ref, given_ref, slope_ref, part):
    _, rows, hidden_dev = plane_ref.shape
    images, width = normed_ref.shape
    half_images = kept_ref.shape[0]
    solved = index_ref.shape[1]
    half = solved // 2
    up_pre = dot32(normed_ref[...], plane_ref[:, : rows // 2, :].reshape(width, hidden_dev))
    activ, slope = gelu_parts(up_pre)
    slope_ref[...] = slope
    down_t = plane_ref[:, rows // 2 :, :].reshape(width, hidden_dev)
    part[...] = dot_t(activ.astype(BF16), down_t)
    core = flag_ref[1]
    high = slope.astype(BF16)
    low = (slope - high.astype(F32)).astype(BF16)
    pick = (lax.broadcasted_iota(jnp.int32, (hidden_dev, solved), 0) == index_ref[...]).astype(BF16)
    gain = dot32(jnp.concatenate([high, low], axis=0), pick)
    gain = jnp.where(core == 0, (gain[:images] + gain[images:]) * picked_ref[:, :solved], 0.0)
    for out, side, at in ((kept_ref, core, 0), (given_ref, 1 - core, half)):
        rows_here = pl.ds(pl.multiple_of(side * half_images, half_images), half_images)
        out[:, :width] = part[rows_here, :]
        out[:, width : width + half] = gain[:half_images, at : at + half]
        out[:, width + half :] = gain[half_images:, at : at + half]


def split2(values):
    high = lax.reduce_precision(values, 8, 7)
    return high.astype(BF16), (values - high).astype(BF16)


def dot32(lhs, rhs):
    return jnp.dot(lhs, rhs, preferred_element_type=F32)


def dot_t(lhs, rhs):
    return lax.dot_general(lhs, rhs, (((1,), (1,)), ((), ())), preferred_element_type=F32)


def dot_split(values, rhs):
    rows = values.shape[0]
    both = dot32(jnp.concatenate(split2(values), axis=0), rhs)
    return both[:rows] + both[rows:]


def one_hot(index, depth):
    return (lax.broadcasted_iota(jnp.int32, (depth, index.shape[0]), 0) == index[None, :]).astype(BF16)


def solved_kernel(extra_ref, down_ref):
    width, half = down_ref.shape
    places, sub, lanes = extra_ref.shape
    parts = width // (places * sub)
    at = lanes - (parts + 1) * half
    for place in range(places):
        for b in range(parts):
            row = (place * parts + b) * sub
            down_ref[row : row + sub, :] = extra_ref[place, :, at + b * half : at + (b + 1) * half]


def middle_kernel(
    flag_ref, mine_ref, theirs_ref, head_ref, down_ref, down0_ref, down1_ref, inv_ref, share_ref, own_ref, mix_ref
):
    half_images = mine_ref.shape[0]
    width = head_ref.shape[1]
    images = 2 * half_images
    half = down0_ref.shape[1]
    logits = head_ref.shape[0] // 4
    first_core = flag_ref[1] == 0
    mine, theirs = mine_ref[:, :width], theirs_ref[:, :width]
    for side, source in ((flag_ref[1], mine_ref), (1 - flag_ref[1], theirs_ref)):
        mix_ref[side, :half_images, :] = source[:, width : width + half]
        mix_ref[side, half_images:images, :] = source[:, width + half :]
    block = jnp.concatenate([jnp.where(first_core, mine, theirs), jnp.where(first_core, theirs, mine)], axis=0)
    centred = block - jnp.mean(block, axis=1, keepdims=True)
    inv_std = lax.rsqrt(jnp.mean(centred * centred, axis=1, keepdims=True) + 1e-06)
    xhat = centred * inv_std
    inv_ref[...] = inv_std
    high = xhat.astype(BF16)
    low = (xhat - high.astype(F32)).astype(BF16)
    head = head_ref[...]
    both = jnp.concatenate([high, low], axis=0)
    share = dot_t(both, head[2 * logits :])
    share = share[:images] + share[images:]
    share_ref[...] = (share[:, :logits] + share[:, logits:]) / width
    lhs = jnp.concatenate([both, head[: 2 * logits]], axis=0)

    def write(rhs_ref, put):
        product = dot32(lhs, rhs_ref[...])
        tail = product[2 * images :]
        put(slice(0, images), product[:images] + product[images : 2 * images])
        put(slice(images, images + logits), tail[:logits] + tail[logits:])

    def put_own(rows, values):
        own_ref[rows, :] = values

    def put_mine(rows, values):
        mix_ref[flag_ref[1], images + rows.start : images + rows.stop, :] = values

    def put_theirs(rows, values):
        mix_ref[1 - flag_ref[1], images + rows.start : images + rows.stop, :] = values

    write(down_ref, put_own)
    write(down0_ref, put_mine)
    write(down1_ref, put_theirs)


def last_kernel(flag_ref, gain_ref, inv_ref, share_ref, own_ref, mix_ref, inverse_ref, extra_ref, out_ref):
    images = gain_ref.shape[0]
    logits = share_ref.shape[1]
    panel = inverse_ref.shape[1]
    first_image = pl.multiple_of(pl.program_id(0) * STEP, STEP)
    here = pl.ds(first_image, STEP)
    inv_std = inv_ref[here, :]
    diagonal = lax.broadcasted_iota(jnp.int32, (1, logits, logits), 1) == lax.broadcasted_iota(
        jnp.int32, (1, logits, logits), 2
    )
    share = jnp.sum(jnp.where(diagonal, share_ref[here, :][:, None, :], 0.0), axis=2, keepdims=True)

    def jacobian(gain, along, head):
        scale = gain * inv_std
        values = scale[:, None, :] * head[None] - share * (scale * along)[:, None, :]
        return values.reshape(STEP * logits, values.shape[2])

    def solved_side(side):
        along = mix_ref[side, pl.ds(images + first_image, STEP), :]
        return jacobian(mix_ref[side, here, :], along, mix_ref[side, 2 * images : 2 * images + logits, :])

    def inverted(values, inverse):
        return dot_t(values.astype(BF16), inverse).astype(BF16)

    first = inverted(solved_side(0), inverse_ref[0])
    rows_dev = gain_ref.shape[1]
    panel_01 = extra_ref[:, :, extra_ref.shape[2] - panel :].reshape(panel, panel)
    second = inverted(solved_side(1) - dot32(first, panel_01), inverse_ref[1])
    own = jacobian(gain_ref[here, :], own_ref[here, :], own_ref[images : images + logits, :])
    panel_0 = extra_ref[:, :, :rows_dev].reshape(panel, rows_dev)
    panel_1 = extra_ref[:, :, rows_dev : 2 * rows_dev].reshape(panel, rows_dev)
    below = (own - (dot32(first, panel_0) + dot32(second, panel_1))).astype(BF16)
    out_ref[...] = below.reshape(out_ref.shape)

    @pl.when(flag_ref[0] == 1)
    def _():
        out_ref[:, :, :panel] = first.reshape(STEP, logits, panel)
        out_ref[:, :, panel : 2 * panel] = second.reshape(STEP, logits, panel)


def body(normed, residual_in, w_up, w_down, final_gain, head_cols, sub_inputs, sub_hidden, panels, inverses):
    images, width = normed.shape
    own, hidden_dev = w_up.shape
    logits = head_cols.shape[1]
    panel = inverses.shape[1]
    panel_dev = panels.shape[1]
    rows_dev = sub_inputs.shape[0]
    z_hi, core = lax.axis_index("zh"), lax.axis_index("c")
    rank = z_hi * 2 + core
    local_hidden = sub_hidden - rank * hidden_dev
    half = panel
    vmem = pl.BlockSpec(memory_space=pltpu.VMEM)
    smem = pl.BlockSpec(memory_space=pltpu.SMEM)
    flag = jnp.stack([jnp.where(rank == 0, 1, 0), core, lax.axis_index("zl")]).astype(jnp.int32)

    both = jnp.concatenate([w_up, w_down.T], axis=0)
    line = gather_by_sends(both, "zl", 4)
    line = pl.pallas_call(
        weights_kernel,
        out_shape=jax.ShapeDtypeStruct((16, 8 * own, hidden_dev), BF16),
        in_specs=[vmem],
        out_specs=vmem,
        compiler_params=LIMIT,
        name="merge_weights",
    )(line)
    plane = lax.all_to_all(line, ("x", "y"), 0, 0)

    pick_first = one_hot(local_hidden[: 2 * panel], hidden_dev)
    chosen = dot32(both[own:], pick_first).astype(BF16)
    block01 = panels[0][:, panel : 2 * panel]
    chosen = [jnp.concatenate([chosen[:, at : at + half], block01], axis=0) for at in (0, half)]
    payload = jnp.where(core == 0, chosen[0], lax.ppermute(chosen[1], "c", [(0, 1)]))
    payload = jnp.where(z_hi == 1, lax.ppermute(payload, "zh", [(0, 1)]), payload)
    payload = jnp.where(z_hi >= 2, lax.ppermute(payload, "zh", [(0, 3), (1, 2)]), payload)

    chunks = rows_dev // half
    narrow = panels.reshape(2 * panel_dev * chunks, half)
    narrow = jnp.concatenate([narrow, payload], axis=0)
    pieces = ring_pieces(narrow, "zl", 4)
    device, source = [], []
    for q in range(2):
        for b in range(chunks):
            device += [r // panel_dev for r in range(4 * panel_dev)]
            source += [(q * panel_dev + r % panel_dev) * chunks + b for r in range(4 * panel_dev)]
    at = 2 * panel_dev * chunks
    device += [r // own for r in range(4 * own)] + [r // panel_dev for r in range(4 * panel_dev)]
    source += [at + r % own for r in range(4 * own)] + [at + own + r % panel_dev for r in range(4 * panel_dev)]
    extra = pl.pallas_call(
        extra_kernel,
        out_shape=jax.ShapeDtypeStruct((16, 16, len(device) // 16 * half), BF16),
        in_specs=[smem] + [vmem] * 6,
        out_specs=pl.BlockSpec(memory_space=pltpu.HBM),
        scratch_shapes=[pltpu.VMEM((16, len(device) // 16 * half), BF16), pltpu.SemaphoreType.DMA((16,))],
        compiler_params=LARGE,
        name="merge_extra",
    )(flag, np.array(device, np.int32)[:, None], np.array(source, np.int32)[:, None], *pieces)
    extra = lax.all_to_all(extra, ("x", "y"), 0, 0)

    mine = jnp.where(core == 0, residual_in[: images // 2], residual_in[images // 2 :]).astype(F32)
    mine = jnp.pad(mine, ((0, 0), (0, 2 * half)))

    picked = dot32(normed, one_hot(sub_inputs, width))
    kept, given, slope = pl.pallas_call(
        forward_kernel,
        out_shape=(
            jax.ShapeDtypeStruct((images // 2, width + 2 * half), F32),
            jax.ShapeDtypeStruct((images // 2, width + 2 * half), F32),
            jax.ShapeDtypeStruct((images, hidden_dev), F32),
        ),
        in_specs=[smem] + [vmem] * 4,
        out_specs=(vmem,) * 3,
        scratch_shapes=[pltpu.VMEM((images, width), F32)],
        compiler_params=LIMIT,
        name="forward",
    )(flag, normed, plane, local_hidden[None, : 2 * panel], picked)
    pair = kept + swap_core(given)
    is_block = lax.broadcasted_iota(jnp.int32, pair.shape, 1) < width
    near = lax.ppermute(pair.astype(BF16), "zh", [(i, i ^ 1) for i in range(4)]).astype(F32)
    pair = jnp.where(is_block, pair + near, jnp.where(z_hi == 1, near, pair))
    far = lax.ppermute(pair.astype(BF16), "zh", [(i, 3 - i) for i in range(4)]).astype(F32)

    pick_own = one_hot(local_hidden, hidden_dev)
    down_t = plane[:, 4 * own :].reshape(width, hidden_dev)
    down_own = dot32(down_t, pick_own).astype(BF16)
    gain_own = dot_split(slope, pick_own) * picked
    head = final_gain[:, None] * head_cols.astype(F32)
    centred_head = head - jnp.mean(head, axis=0)
    head_parts = jnp.concatenate(split2(centred_head.T) + split2(head.T), axis=0)

    block = jnp.where(is_block, mine + (pair + far), jnp.where(z_hi >= 2, far, pair))
    block_pair = swap_core(block)

    down_mine = pl.pallas_call(
        solved_kernel,
        out_shape=jax.ShapeDtypeStruct((width, half), BF16),
        in_specs=[vmem],
        out_specs=vmem,
        compiler_params=LIMIT,
        name="solved",
    )(extra)
    down_theirs = swap_core(down_mine)
    inv_std, share, own_products, mix = pl.pallas_call(
        middle_kernel,
        out_shape=(
            jax.ShapeDtypeStruct((images, 1), F32),
            jax.ShapeDtypeStruct((images, logits), F32),
            jax.ShapeDtypeStruct((images + logits, rows_dev), F32),
            jax.ShapeDtypeStruct((2, 2 * images + logits, half), F32),
        ),
        in_specs=[smem] + [vmem] * 6,
        out_specs=(vmem,) * 4,
        compiler_params=LIMIT,
        name="middle",
    )(flag, block, block_pair, head_parts, down_own, down_mine, down_theirs)
    return pl.pallas_call(
        last_kernel,
        grid=(images // STEP,),
        out_shape=jax.ShapeDtypeStruct((images, logits, rows_dev), BF16),
        in_specs=[smem] + [vmem] * 7,
        out_specs=pl.BlockSpec((STEP, logits, rows_dev), lambda i: (i, 0, 0)),
        compiler_params=LIMIT,
        name="last",
    )(flag, gain_own, inv_std, share, own_products, mix, inverses, extra)


def solution(mesh):
    fine = Mesh(mesh.devices.reshape(4, 4, 4, 4, 2), ("x", "y", "zl", "zh", "c"))
    in_specs = (
        P(DP, None),
        P(DP, None),
        P(DP, TENSOR),
        P(TENSOR, DP),
        P(),
        P(),
        P(TENSOR),
        P(TENSOR),
        P(None, DP, TENSOR),
        P(),
    )
    out_specs = P(DP, None, TENSOR)

    return jax.shard_map(body, mesh=fine, in_specs=in_specs, out_specs=out_specs, check_vma=False)
```
